32 devices in a mesh: groups: 2 (over y), row: 4 (over z), col: 2 (over x), chan: 2 (over core).
Axes of the slice: x: 2, y: 2, z: 4, core: 2. Of those that a mesh axis runs over, the one named last changes fastest.
Arguments:
- pair_input: bfloat16 [512, 256, 128], P(('groups', 'row'), ('col', 'chan')), parts along dimension 0, may hold values from -6 to 6
- alignment_features: bfloat16 [128, 512, 64], P('row', ('groups', 'col', 'chan')), parts along dimension 1, may hold values from -6 to 6
- alignment_mask: int32 [128, 512], P('row', ('groups', 'col', 'chan')), parts along dimension 1, may hold values from 0 to 1
- token_valid: int32 [512], P('groups'), parts along dimension 0, may hold values from 0 to 1, as said below
- left_weight: bfloat16 [64, 32], replicated, may hold values from -0.75 to 0.75
- right_weight: bfloat16 [64, 32], replicated, may hold values from -0.75 to 0.75
- output_weight: bfloat16 [1024, 128], replicated, may hold values from -1.75 to 1.75
- gate_weight: bfloat16 [128, 512], replicated, may hold values from -0.5 to 0.5
- up_weight: bfloat16 [128, 512], replicated, may hold values from -0.5 to 0.5
- down_weight: bfloat16 [512, 128], replicated, may hold values from -0.25 to 0.25
- kernel_weight: bfloat16 [3, 3, 128, 128], replicated, may hold values from -0.1875 to 0.1875
Outputs:
- pair_out: bfloat16 [512, 256, 128], P(('groups', 'row'), ('col', 'chan')), parts along dimension 0
The draws below stay inside these ranges and needn't reach their ends.
There are 2 independent parts, one for each index of `groups`. The reference program is written for one: setup_inputs(seed, part) draws one part's arguments, and reference() takes and returns one part's arrays. A program takes and returns all parts, laid end to end along the dimension named above; an argument that names none is the same for every part. Nothing has to cross between parts.
Inputs may be any that keep to these rules, and one draw needn't show every extreme that they name: `token_valid`: the ones come first.
All inputs are finite; a program needn't handle non-finite values.
Results may differ from the reference program's by a relative error of at most 0.014.
Values may be sent and summed in bfloat16 or wider, within the bound.
A program may use at most 64 MiB of HBM per device.

```python
import jax
import jax.numpy as jnp
from jax import lax

CPAIR = 128
ALIGN_CHANNELS = 64
COPM = 32
CHID = 512
TOKEN_COUNT = 256
ALIGN_ROWS = 128


def draw_alignment_mask(key, part):
    key_cover, key_vacant, key_keep = jax.random.split(jax.random.fold_in(key, 101), 3)
    coverage = jax.random.randint(key_cover, (TOKEN_COUNT,), ALIGN_ROWS // 2, ALIGN_ROWS + 1)
    vacant = jax.random.randint(key_vacant, (TOKEN_COUNT,), 0, 64)
    coverage = jnp.where(vacant == 0, 0, coverage)
    retained = jax.random.randint(key_keep, (ALIGN_ROWS, TOKEN_COUNT), 0, 8)
    seq_rows = jnp.arange(ALIGN_ROWS)[:, None]
    return ((seq_rows < coverage[None, :]) & (retained > 0)).astype(jnp.int32)


def draw_token_valid(key, part):
    length_key = jax.random.fold_in(key, 202)
    filled = jax.random.randint(length_key, (), TOKEN_COUNT - TOKEN_COUNT // 8, TOKEN_COUNT + 1)
    return (jnp.arange(TOKEN_COUNT) < filled).astype(jnp.int32)


def shard_levels(own_key, shape, cuts, low, largest):
    factor_of, own = 1.0, jax.random.fold_in(own_key, 6)
    for axis_at, shards_of in cuts:
        heights = jnp.exp(jax.random.uniform(jax.random.fold_in(own, axis_at), (shards_of,), jnp.float32, low / len(cuts), largest / len(cuts)))
        factor_of = factor_of * jnp.repeat(heights, shape[axis_at] // shards_of).reshape([-1 if axis == axis_at else 1 for axis in range(len(shape))])
    return factor_of


def bell_draw(stream_key, shape, deviation, reach, cuts=(), held_as=jnp.bfloat16):
    values = deviation * jax.random.normal(stream_key, shape, jnp.float32)
    if cuts:
        values = values * shard_levels(stream_key, shape, cuts, -0.22, 0.18)
    return jnp.clip(values, -reach, reach).astype(held_as)


def setup_inputs(seed: int = 0, part: int = 0) -> dict:
    splits = jax.random.split(jax.random.key(seed), 12)
    part_splits = jax.random.split(jax.random.fold_in(splits[11], part), 12)
    pair_input = bell_draw(part_splits[0], (TOKEN_COUNT, TOKEN_COUNT, CPAIR), 1.0, 6.0, ((0, 4), (1, 4)))
    alignment_features = bell_draw(part_splits[1], (ALIGN_ROWS, TOKEN_COUNT, ALIGN_CHANNELS), 1.0, 6.0, ((0, 4), (1, 4)))
    alignment_mask = draw_alignment_mask(jax.random.fold_in(jax.random.fold_in(splits[11], part), 71), part)
    token_valid = draw_token_valid(jax.random.fold_in(jax.random.fold_in(splits[11], part), 71), part)
    left_weight = bell_draw(splits[4], (ALIGN_CHANNELS, COPM), ALIGN_CHANNELS ** -0.5, 0.75)
    right_weight = bell_draw(splits[5], (ALIGN_CHANNELS, COPM), ALIGN_CHANNELS ** -0.5, 0.75)
    output_weight = bell_draw(splits[6], (COPM * COPM, CPAIR), 0.3, 1.75)
    gate_weight = bell_draw(splits[7], (CPAIR, CHID), CPAIR ** -0.5, 0.5)
    up_weight = bell_draw(splits[8], (CPAIR, CHID), CPAIR ** -0.5, 0.5)
    down_weight = bell_draw(splits[9], (CHID, CPAIR), CHID ** -0.5, 0.25)
    kernel_weight = bell_draw(splits[10], (3, 3, CPAIR, CPAIR), (9 * CPAIR) ** -0.5, 0.1875)
    return {"pair_input": pair_input, "alignment_features": alignment_features, "alignment_mask": alignment_mask, "token_valid": token_valid, "left_weight": left_weight, "right_weight": right_weight, "output_weight": output_weight, "gate_weight": gate_weight, "up_weight": up_weight, "down_weight": down_weight, "kernel_weight": kernel_weight}


epsilon = 1e-05
strip_rows = 16
slab_rows = 4096

def transition(pair_rows, gate_weight, up_weight, down_weight):
    values = pair_rows.astype(jnp.float32)
    centre = lax.optimization_barrier(jnp.mean(values, axis=-1, keepdims=True))
    spread = lax.optimization_barrier(jnp.mean(jnp.square(values - centre), axis=-1, keepdims=True))
    normed = ((values - centre) * lax.rsqrt(spread + epsilon)).astype(jnp.bfloat16)
    gate_act = jnp.dot(normed, gate_weight, preferred_element_type=jnp.float32)
    up_act = jnp.dot(normed, up_weight, preferred_element_type=jnp.float32)
    hidden = (jax.nn.silu(gate_act) * up_act).astype(jnp.bfloat16)
    return (values + jnp.dot(hidden, down_weight, preferred_element_type=jnp.float32)).astype(jnp.bfloat16)

def reference(pair_input, alignment_features, alignment_mask, token_valid, left_weight, right_weight, output_weight, gate_weight, up_weight, down_weight, kernel_weight):
    real_mask = alignment_mask.astype(jnp.float32)
    alignment_real = alignment_features.astype(jnp.float32)
    left_projected = (jnp.einsum('vdi,ie->vde', alignment_real, left_weight.astype(jnp.float32)) * real_mask[:, :, None]).astype(jnp.bfloat16)
    right_projected = (jnp.einsum('vdi,ie->vde', alignment_real, right_weight.astype(jnp.float32)) * real_mask[:, :, None]).astype(jnp.bfloat16)
    counts = jnp.dot(real_mask.T, real_mask, precision=lax.Precision.HIGHEST, preferred_element_type=jnp.float32)
    right_flat = right_projected.reshape(ALIGN_ROWS, TOKEN_COUNT * COPM)

    def outer_rows(first_row):
        left_part = lax.dynamic_slice_in_dim(left_projected, first_row, strip_rows, 1).reshape(ALIGN_ROWS, strip_rows * COPM)
        products = jnp.dot(left_part.T, right_flat, preferred_element_type=jnp.float32)
        products = products.reshape(strip_rows, COPM, TOKEN_COUNT, COPM).transpose(0, 2, 1, 3)
        products = products.reshape(strip_rows * TOKEN_COUNT, COPM * COPM).astype(jnp.bfloat16)
        update = jnp.dot(products, output_weight, preferred_element_type=jnp.float32).reshape(strip_rows, TOKEN_COUNT, CPAIR)
        pair_count = lax.dynamic_slice_in_dim(counts, first_row, strip_rows, 0)
        update = update / jnp.maximum(pair_count, 1.0)[:, :, None]
        base_pair = lax.dynamic_slice_in_dim(pair_input, first_row, strip_rows, 0).astype(jnp.float32)
        return (base_pair + update).astype(jnp.bfloat16)
    starts = jnp.arange(TOKEN_COUNT // strip_rows, dtype=jnp.int32) * strip_rows
    pair_one = lax.map(outer_rows, starts).reshape(TOKEN_COUNT, TOKEN_COUNT, CPAIR)

    def one_slab(pair_slab):
        return transition(pair_slab, gate_weight, up_weight, down_weight)
    pair_slabs = pair_one.reshape(TOKEN_COUNT * TOKEN_COUNT // slab_rows, slab_rows, CPAIR)
    pair_two = lax.map(one_slab, pair_slabs).reshape(TOKEN_COUNT, TOKEN_COUNT, CPAIR)
    pair_mirror = jnp.swapaxes(pair_two, 0, 1)
    pad_real = token_valid.astype(jnp.float32)
    symmetric = (pair_two.astype(jnp.float32) + pair_mirror.astype(jnp.float32)) * 0.5
    masked = (symmetric * pad_real[:, None, None] * pad_real[None, :, None]).astype(jnp.bfloat16)
    padded = jnp.pad(masked, ((1, 1), (1, 1), (0, 0)))

    def conv_rows(first_row):
        window = lax.dynamic_slice_in_dim(padded, first_row, strip_rows + 2, 0)
        summed = jnp.zeros((strip_rows * TOKEN_COUNT, CPAIR), jnp.float32)
        for shift_row in range(3):
            for shift_col in range(3):
                shifted = window[shift_row:shift_row + strip_rows, shift_col:shift_col + TOKEN_COUNT].reshape(strip_rows * TOKEN_COUNT, CPAIR)
                summed = summed + jnp.dot(shifted, kernel_weight[shift_row, shift_col], preferred_element_type=jnp.float32)
        centre = lax.dynamic_slice_in_dim(symmetric, first_row, strip_rows, 0).reshape(strip_rows * TOKEN_COUNT, CPAIR)
        return (centre + summed).astype(jnp.bfloat16).reshape(strip_rows, TOKEN_COUNT, CPAIR)
    return lax.map(conv_rows, starts).reshape(TOKEN_COUNT, TOKEN_COUNT, CPAIR)
```

```python
import functools

import jax
import jax.numpy as jnp
from jax import lax
from jax.experimental import pallas as pl
from jax.experimental.pallas import tpu as pltpu
from jax.sharding import PartitionSpec as P

epsilon = 1e-05
F32, BF16 = jnp.float32, jnp.bfloat16
MESH = pl.DeviceIdType.MESH
AROUND = [(a, b) for a in (-1, 0, 1) for b in (-1, 0, 1) if (a, b) != (0, 0)]


def dot(a, b):
    return jnp.dot(a, b, preferred_element_type=F32)


def block_kernel(
    sizes,
    pair_ref,
    feat_ref,
    mask_ref,
    valid_ref,
    wl_ref,
    wr_ref,
    wo_ref,
    wg_ref,
    wu_ref,
    wd_ref,
    wk_ref,
    out_ref,
    lsend,
    lg,
    rg,
    rt,
    rq,
    lcat,
    wof,
    w4,
    zs,
    rexp,
    ones,
    two,
    mirror,
    mf,
    sym,
    wide,
    colf,
    hsend,
    hrecv,
    l1_send,
    l1_recv,
    l2_send,
    l2_recv,
    r_send,
    r_recv,
    m_send,
    m_recv,
    h_send,
    h_recv,
):
    rn, cn, chans, fold, rd, cd, ch, sl, tl, pw, cr = sizes
    row = lax.axis_index("row")
    col = lax.axis_index("col") * chans + lax.axis_index("chan")
    per = 128 // pw
    lgroups, rgroups = rd // per, cd // per
    depth = rn * sl
    steps = rd // cr
    cgroups = cr // per

    def at(r, c):
        return {"row": r, "col": c // chans, "chan": c % chans}

    def remote(src, dst, ssem, rsem, r, c):
        return pltpu.make_async_remote_copy(
            src_ref=src, dst_ref=dst, send_sem=ssem, recv_sem=rsem,
            device_id=at(r, c), device_id_type=MESH,
        )

    hrecv[...] = jnp.zeros_like(hrecv)
    barrier = pltpu.get_barrier_semaphore()

    def greet(n, carry):
        pl.semaphore_signal(barrier, inc=1, device_id=at(n // cn, n % cn), device_id_type=MESH)
        return carry

    lax.fori_loop(0, rn * cn, greet, 0)

    aw = wl_ref.shape[0]
    spread = (
        lax.broadcasted_iota(jnp.int32, (pw, 128), 1) % pw
        == lax.broadcasted_iota(jnp.int32, (pw, 128), 0)
    ).astype(F32).astype(BF16)
    own = (
        lax.broadcasted_iota(jnp.int32, (per * aw, 128), 0) // aw
        == lax.broadcasted_iota(jnp.int32, (per * aw, 128), 1) // pw
    )

    def block_weight(w):
        tiled = dot(w, spread)
        return jnp.where(own, jnp.concatenate([tiled] * per, axis=0), 0.0).astype(BF16)

    feats = feat_ref[...]
    left = dot(feats, block_weight(wl_ref[...])).reshape(tl // per, sl, 128).astype(BF16)
    right = dot(feats, block_weight(wr_ref[...])).reshape(tl // per, sl, 128).astype(BF16)
    mask = mask_ref[...].astype(F32).astype(BF16)
    for k in range(fold):
        lsend[k, 0:lgroups] = left[k * lgroups : (k + 1) * lgroups]
        lsend[k, lgroups] = jnp.zeros((sl, 128), BF16)
        lsend[k, lgroups, :, 0:rd] = mask[:, k * rd : (k + 1) * rd]
    rg[row, 0:rgroups] = right
    rg[row, rgroups] = jnp.zeros((sl, 128), BF16)
    rg[row, rgroups, :, 0:tl] = mask

    pl.semaphore_wait(barrier, rn * cn)

    for k in range(fold):
        to_row, to_col = col * fold + k, row % cn
        mine = jnp.logical_and(to_row == row, to_col == col)
        slot = row // cn

        @pl.when(mine)
        def _():
            pltpu.make_async_copy(lsend.at[k], lg.at[row], l1_recv.at[slot]).start()

        @pl.when(jnp.logical_not(mine))
        def _():
            remote(lsend.at[k], lg.at[row], l1_send.at[k], l1_recv.at[slot], to_row, to_col).start()

    for d in range(1, rn):
        remote(
            rg.at[row], rg.at[row], r_send.at[d - 1], r_recv.at[d - 1], (row + d) % rn, col
        ).start()

    wof[...] = wo_ref[...].astype(F32)
    w4[...] = jnp.zeros_like(w4)
    for q in range(pw):
        part = wof[pl.ds(q, pw, stride=pw), :].astype(BF16)
        for i in range(per):
            w4[q * 128 + i * pw : q * 128 + (i + 1) * pw, i * ch : (i + 1) * ch] = part

    for m in range(fold):
        slot = col + m * cn
        pltpu.make_async_copy(lg.at[slot], lg.at[slot], l1_recv.at[m]).wait()
        for d in range(1, cn):
            remote(
                lg.at[slot], lg.at[slot], l2_send.at[m, d - 1], l2_recv.at[m, d - 1],
                row, (col + d) % cn,
            ).start()

    for d in range(1, rn):
        slot = (row + rn - d) % rn
        pltpu.make_async_copy(rg.at[slot], rg.at[slot], r_recv.at[d - 1]).wait()
    for g in range(rgroups):
        slab = rg[:, g].astype(F32).reshape(depth, 128)
        rt[g * 128 : (g + 1) * 128, :] = slab.T
    for q in range(pw):
        rq[q * cd : (q + 1) * cd, :] = rt[pl.ds(q, cd, stride=pw), :].astype(BF16)

    for m in range(fold):
        for d in range(1, cn):
            slot = (col + cn - d) % cn + m * cn
            pltpu.make_async_copy(lg.at[slot], lg.at[slot], l2_recv.at[m, d - 1]).wait()
    for g in range(lgroups):
        slab = lg[:, g].astype(F32).reshape(depth, 128).astype(BF16)
        where = g % cgroups
        lcat[g // cgroups, :, where * 128 : (where + 1) * 128] = slab
    left_mask = lg[:, lgroups].astype(F32).reshape(depth, 128)
    right_mask = rg[:, rgroups].astype(F32).reshape(depth, 128)
    counts = dot(right_mask.T.astype(BF16), left_mask.astype(BF16))
    inverse = 1.0 / jnp.maximum(counts, 1.0)
    for i in range(rd):
        rexp[i] = jnp.broadcast_to(inverse[0:cd, i : i + 1], (cd, ch))

    qstep = min(8, pw)

    def to_mirror(step, k):
        src = two.at[pl.ds(step * cr, cr), pl.ds(k * rd, rd)]
        dst = mirror.at[pl.ds((row % fold) * rd + step * cr, cr)]
        return src, dst

    def one_step(step, carry):
        lpart = lcat[step]
        for q0 in range(0, pw, qstep):
            z = dot(rq[q0 * cd : (q0 + qstep) * cd, :], lpart).astype(BF16)
            for q in range(qstep):
                for g in range(cgroups):
                    zs[g * cd : (g + 1) * cd, (q0 + q) * 128 : (q0 + q + 1) * 128] = z[
                        q * cd : (q + 1) * cd, g * 128 : (g + 1) * 128
                    ]
        update = dot(zs[...], w4[...])
        for g in range(cgroups):
            for i in range(per):
                at_row = step * cr + g * per + i
                add = update[g * cd : (g + 1) * cd, i * ch : (i + 1) * ch] * rexp[at_row]
                ones[g * per + i] = (pair_ref[at_row].astype(F32) + add).astype(BF16)
        half = max(1, cr // 2)
        for h in range(0, cr, half):
            values = ones[h : h + half].reshape(half * cd, ch).astype(F32)
            centre = jnp.mean(values, axis=-1, keepdims=True)
            shifted = values - centre
            var = jnp.mean(jnp.square(shifted), axis=-1, keepdims=True)
            normed = (shifted * lax.rsqrt(var + epsilon)).astype(BF16)
            gate = dot(normed, wg_ref[...])
            up = dot(normed, wu_ref[...])
            hidden = (gate / (1.0 + jnp.exp(-gate)) * up).astype(BF16)
            result = (values + dot(hidden, wd_ref[...])).astype(BF16)
            two[pl.ds(step * cr + h, half)] = result.reshape(half, cd, ch)
        for k in range(fold):
            to_row, to_col = col * fold + k, row // fold
            mine = jnp.logical_and(to_row == row, to_col == col)
            src, dst = to_mirror(step, k)
            rsem = m_recv.at[row % fold, step]

            @pl.when(mine)
            def _():
                pltpu.make_async_copy(src, dst, rsem).start()

            @pl.when(jnp.logical_not(mine))
            def _():
                remote(src, dst, m_send.at[k, step], rsem, to_row, to_col).start()

        return carry

    lax.fori_loop(0, steps, one_step, 0)

    for step in range(steps):
        for k in range(fold):
            piece = mirror.at[pl.ds(k * rd + step * cr, cr)]
            pltpu.make_async_copy(piece, piece, m_recv.at[k, step]).wait()
            begin = k * rd + step * cr
            mf[begin * rd : (begin + cr) * rd, :] = (
                mirror[begin : begin + cr].astype(F32).reshape(cr * rd, ch)
            )

    valid_cols = valid_ref[pl.ds(pl.multiple_of(col * cd, 8), cd), :]

    def one_row(i, carry):
        half_sum = (two[i].astype(F32) + mf[pl.ds(i, cd, stride=rd), :]) * 0.5
        sym[i] = half_sum
        masked = half_sum * valid_cols * valid_ref[pl.ds(row * rd + i, 1), :]
        wide[i + 1, :, ch : 2 * ch] = masked.astype(BF16)
        colf[0, pl.ds(i, 1), :] = masked[0:1]
        colf[1, pl.ds(i, 1), :] = masked[cd - 1 : cd]
        return carry

    lax.fori_loop(0, rd, one_row, 0)

    for n, (a, b) in enumerate(AROUND):
        if b == 0:
            hsend[n, 0:cd] = wide[1 if a < 0 else rd, :, ch : 2 * ch]
        elif a == 0:
            hsend[n, 0:rd] = colf[0 if b < 0 else 1].astype(BF16)
        else:
            corner = colf[0 if b < 0 else 1, 0:1] if a < 0 else colf[0 if b < 0 else 1, rd - 1 : rd]
            hsend[n, 0:16] = jnp.broadcast_to(corner, (16, ch)).astype(BF16)

    def there(a, b):
        r, c = row + a, col + b
        return jnp.logical_and(
            jnp.logical_and(r >= 0, r < rn), jnp.logical_and(c >= 0, c < cn)
        )

    def lines(a, b):
        return cd if b == 0 else (rd if a == 0 else 16)

    for n, (a, b) in enumerate(AROUND):

        @pl.when(there(a, b))
        def _():
            size = lines(a, b)
            remote(
                hsend.at[n, pl.ds(0, size)], hrecv.at[n, pl.ds(0, size)], h_send.at[n],
                h_recv.at[n], row + a, col + b,
            ).start()

    for n, (a, b) in enumerate(AROUND):

        @pl.when(there(-a, -b))
        def _():
            piece = hrecv.at[n, pl.ds(0, lines(a, b))]
            pltpu.make_async_copy(piece, piece, h_recv.at[n]).wait()

    slot_of = {direction: n for n, direction in enumerate(AROUND)}
    wide[0, :, ch : 2 * ch] = hrecv[slot_of[(1, 0)], 0:cd]
    wide[rd + 1, :, ch : 2 * ch] = hrecv[slot_of[(-1, 0)], 0:cd]
    colf[0] = hrecv[slot_of[(0, 1)], 0:rd].astype(F32)
    colf[1] = hrecv[slot_of[(0, -1)], 0:rd].astype(F32)
    place = lax.broadcasted_iota(jnp.int32, (cd, ch), 0)

    def widen(i, before, after):
        centre = wide[i, :, ch : 2 * ch].astype(F32)
        wide[i, :, 0:ch] = jnp.where(place == 0, before, pltpu.roll(centre, 1, 0)).astype(BF16)
        wide[i, :, 2 * ch : 3 * ch] = jnp.where(
            place == cd - 1, after, pltpu.roll(centre, cd - 1, 0)
        ).astype(BF16)

    def widen_row(i, carry):
        widen(i + 1, colf[0, pl.ds(i, 1), :], colf[1, pl.ds(i, 1), :])
        return carry

    lax.fori_loop(0, rd, widen_row, 0)
    widen(
        0,
        hrecv[slot_of[(1, 1)], 0:16].astype(F32)[0:1],
        hrecv[slot_of[(1, -1)], 0:16].astype(F32)[0:1],
    )
    widen(
        rd + 1,
        hrecv[slot_of[(-1, 1)], 0:16].astype(F32)[0:1],
        hrecv[slot_of[(-1, -1)], 0:16].astype(F32)[0:1],
    )

    strip = 8

    def conv(n, carry):
        total = sym[pl.ds(n * strip, strip)].reshape(strip * cd, ch)
        for a in range(3):
            window = wide[pl.ds(n * strip + a, strip)].reshape(strip * cd, 3 * ch)
            total = total + dot(window, wk_ref[a])
        out_ref[pl.ds(n * strip, strip)] = total.astype(BF16).reshape(strip, cd, ch)
        return carry

    lax.fori_loop(0, rd // strip, conv, 0)

    for k in range(fold):
        to_row, to_col = col * fold + k, row % cn

        @pl.when(jnp.logical_not(jnp.logical_and(to_row == row, to_col == col)))
        def _():
            pltpu.make_async_copy(lsend.at[k], lsend.at[k], l1_send.at[k]).wait()

        to_row, to_col = col * fold + k, row // fold

        @pl.when(jnp.logical_not(jnp.logical_and(to_row == row, to_col == col)))
        def _():
            for step in range(steps):
                src, _dst = to_mirror(step, k)
                pltpu.make_async_copy(src, src, m_send.at[k, step]).wait()

    for d in range(1, rn):
        pltpu.make_async_copy(rg.at[row], rg.at[row], r_send.at[d - 1]).wait()
    for m in range(fold):
        for d in range(1, cn):
            slot = col + m * cn
            pltpu.make_async_copy(lg.at[slot], lg.at[slot], l2_send.at[m, d - 1]).wait()
    for n, (a, b) in enumerate(AROUND):

        @pl.when(there(a, b))
        def _():
            piece = hsend.at[n, pl.ds(0, lines(a, b))]
            pltpu.make_async_copy(piece, piece, h_send.at[n]).wait()


def on_device(
    mesh_shape,
    pair_input,
    alignment_features,
    alignment_mask,
    token_valid,
    left_weight,
    right_weight,
    output_weight,
    gate_weight,
    up_weight,
    down_weight,
    kernel_weight,
):
    rd, cd, ch = pair_input.shape
    sl, tl, aw = alignment_features.shape
    pw = left_weight.shape[1]
    hid = gate_weight.shape[1]
    rn, chans = mesh_shape["row"], mesh_shape["chan"]
    cn = mesh_shape["col"] * chans
    fold = rn // cn
    per = 128 // pw
    cr = min(16, rd)
    depth = rn * sl
    steps = rd // cr
    tall = max(rd, cd, 16)
    feats = jnp.where((alignment_mask != 0)[:, :, None], alignment_features, 0)
    feats = feats.reshape(sl, tl // per, per * aw).transpose(1, 0, 2).reshape(-1, per * aw)
    valid = jnp.broadcast_to(token_valid.astype(F32)[:, None], (token_valid.shape[0], ch))
    wk = kernel_weight.reshape(3, 3 * ch, ch)
    sizes = (rn, cn, chans, fold, rd, cd, ch, sl, tl, pw, cr)
    dma = pltpu.SemaphoreType.DMA
    vmem = pl.BlockSpec(memory_space=pltpu.VMEM)
    return pl.pallas_call(
        functools.partial(block_kernel, sizes),
        out_shape=jax.ShapeDtypeStruct((rd, cd, ch), BF16),
        in_specs=[vmem] * 11,
        out_specs=vmem,
        scratch_shapes=[
            pltpu.VMEM((fold, rd // per + 1, sl, 128), BF16),
            pltpu.VMEM((rn, rd // per + 1, sl, 128), BF16),
            pltpu.VMEM((rn, cd // per + 1, sl, 128), BF16),
            pltpu.VMEM((cd * pw, depth), F32),
            pltpu.VMEM((pw * cd, depth), BF16),
            pltpu.VMEM((steps, depth, cr * pw), BF16),
            pltpu.VMEM((pw * pw, ch), F32),
            pltpu.VMEM((pw * 128, per * ch), BF16),
            pltpu.VMEM((cr // per * cd, pw * 128), BF16),
            pltpu.VMEM((rd, cd, ch), F32),
            pltpu.VMEM((cr, cd, ch), BF16),
            pltpu.VMEM((rd, cd, ch), BF16),
            pltpu.VMEM((cd, rd, ch), BF16),
            pltpu.VMEM((cd * rd, ch), F32),
            pltpu.VMEM((rd, cd, ch), F32),
            pltpu.VMEM((rd + 2, cd, 3 * ch), BF16),
            pltpu.VMEM((2, rd, ch), F32),
            pltpu.VMEM((8, tall, ch), BF16),
            pltpu.VMEM((8, tall, ch), BF16),
            dma((fold,)),
            dma((fold,)),
            dma((fold, cn - 1)),
            dma((fold, cn - 1)),
            dma((rn - 1,)),
            dma((rn - 1,)),
            dma((fold, steps)),
            dma((fold, steps)),
            dma((8,)),
            dma((8,)),
        ],
        compiler_params=pltpu.CompilerParams(
            collective_id=0, has_side_effects=True, vmem_limit_bytes=60 * 1024 * 1024
        ),
    )(
        pair_input,
        feats,
        alignment_mask,
        valid,
        left_weight,
        right_weight,
        output_weight,
        gate_weight,
        up_weight,
        down_weight,
        wk,
    )


def solution(mesh):
    placed = (
        P(("groups", "row"), ("col", "chan"), None),
        P("row", ("groups", "col", "chan"), None),
        P("row", ("groups", "col", "chan")),
        P("groups"),
        P(),
        P(),
        P(),
        P(),
        P(),
        P(),
        P(),
    )
    return jax.shard_map(
        functools.partial(on_device, dict(mesh.shape)),
        mesh=mesh,
        in_specs=placed,
        out_specs=P(("groups", "row"), ("col", "chan"), None),
        check_vma=False,
    )
```

```python
import functools

import jax
import jax.numpy as jnp
from jax import lax
from jax.experimental import pallas as pl
from jax.experimental.pallas import tpu as pltpu
from jax.sharding import PartitionSpec as P

epsilon = 1e-05
F32, BF16 = jnp.float32, jnp.bfloat16
MESH = pl.DeviceIdType.MESH
AROUND = [(a, b) for a in (-1, 0, 1) for b in (-1, 0, 1) if (a, b) != (0, 0)]


def dot(a, b):
    return jnp.dot(a, b, preferred_element_type=F32)


def block_kernel(
    sizes,
    pair_ref,
    feat_ref,
    mask_ref,
    valid_ref,
    wl_ref,
    wr_ref,
    wo_ref,
    wg_ref,
    wu_ref,
    wd_ref,
    wk_ref,
    out_ref,
    lsend,
    lg,
    rg,
    rt,
    rq,
    lcat,
    wof,
    w4,
    zs,
    rexp,
    ones,
    two,
    mirror,
    mf,
    sym,
    wide,
    colf,
    hsend,
    hrecv,
    l1_send,
    l1_recv,
    l2_send,
    l2_recv,
    r_send,
    r_recv,
    m_send,
    m_recv,
    relay,
    rl_send,
    rl_recv,
    h_send,
    h_recv,
):
    rn, cn, chans, fold, rd, cd, ch, sl, tl, pw, cr = sizes
    row = lax.axis_index("row")
    col = lax.axis_index("col") * chans + lax.axis_index("chan")
    per = 128 // pw
    lgroups, rgroups = rd // per, cd // per
    depth = rn * sl
    steps = rd // cr
    cgroups = cr // per

    def at(r, c):
        return {"row": r, "col": c // chans, "chan": c % chans}

    def remote(src, dst, ssem, rsem, r, c):
        return pltpu.make_async_remote_copy(
            src_ref=src, dst_ref=dst, send_sem=ssem, recv_sem=rsem,
            device_id=at(r, c), device_id_type=MESH,
        )

    hrecv[...] = jnp.zeros_like(hrecv)
    barrier = pltpu.get_barrier_semaphore()

    def greet(n, carry):
        pl.semaphore_signal(barrier, inc=1, device_id=at(n // cn, n % cn), device_id_type=MESH)
        return carry

    lax.fori_loop(0, rn * cn, greet, 0)

    aw = wl_ref.shape[0]
    spread = (
        lax.broadcasted_iota(jnp.int32, (pw, 128), 1) % pw
        == lax.broadcasted_iota(jnp.int32, (pw, 128), 0)
    ).astype(F32).astype(BF16)
    own = (
        lax.broadcasted_iota(jnp.int32, (per * aw, 128), 0) // aw
        == lax.broadcasted_iota(jnp.int32, (per * aw, 128), 1) // pw
    )

    def block_weight(w):
        tiled = dot(w, spread)
        return jnp.where(own, jnp.concatenate([tiled] * per, axis=0), 0.0).astype(BF16)

    feats = feat_ref[...]
    left = dot(feats, block_weight(wl_ref[...])).reshape(tl // per, sl, 128).astype(BF16)
    right = dot(feats, block_weight(wr_ref[...])).reshape(tl // per, sl, 128).astype(BF16)
    mask = mask_ref[...].astype(F32).astype(BF16)
    for k in range(fold):
        lsend[k, 0:lgroups] = left[k * lgroups : (k + 1) * lgroups]
        lsend[k, lgroups] = jnp.zeros((sl, 128), BF16)
        lsend[k, lgroups, :, 0:rd] = mask[:, k * rd : (k + 1) * rd]
    rg[row, 0:rgroups] = right
    rg[row, rgroups] = jnp.zeros((sl, 128), BF16)
    rg[row, rgroups, :, 0:tl] = mask

    pl.semaphore_wait(barrier, rn * cn)

    for k in range(fold):
        to_row, to_col = col * fold + k, row % cn
        mine = jnp.logical_and(to_row == row, to_col == col)
        slot = row // cn

        @pl.when(mine)
        def _():
            pltpu.make_async_copy(lsend.at[k], lg.at[row], l1_recv.at[slot]).start()

        @pl.when(jnp.logical_not(mine))
        def _():
            remote(lsend.at[k], lg.at[row], l1_send.at[k], l1_recv.at[slot], to_row, to_col).start()

    for d in range(1, rn):
        remote(
            rg.at[row], rg.at[row], r_send.at[d - 1], r_recv.at[d - 1], (row + d) % rn, col
        ).start()

    wof[...] = wo_ref[...].astype(F32)
    w4[...] = jnp.zeros_like(w4)
    for q in range(pw):
        part = wof[pl.ds(q, pw, stride=pw), :].astype(BF16)
        for i in range(per):
            w4[q * 128 + i * pw : q * 128 + (i + 1) * pw, i * ch : (i + 1) * ch] = part

    for m in range(fold):
        slot = col + m * cn
        pltpu.make_async_copy(lg.at[slot], lg.at[slot], l1_recv.at[m]).wait()
        for d in range(1, cn):
            remote(
                lg.at[slot], lg.at[slot], l2_send.at[m, d - 1], l2_recv.at[m, d - 1],
                row, (col + d) % cn,
            ).start()

    for d in range(1, rn):
        slot = (row + rn - d) % rn
        pltpu.make_async_copy(rg.at[slot], rg.at[slot], r_recv.at[d - 1]).wait()
    for g in range(rgroups):
        slab = rg[:, g].astype(F32).reshape(depth, 128)
        rt[g * 128 : (g + 1) * 128, :] = slab.T
    for q in range(pw):
        rq[q * cd : (q + 1) * cd, :] = rt[pl.ds(q, cd, stride=pw), :].astype(BF16)

    for m in range(fold):
        for d in range(1, cn):
            slot = (col + cn - d) % cn + m * cn
            pltpu.make_async_copy(lg.at[slot], lg.at[slot], l2_recv.at[m, d - 1]).wait()
    for g in range(lgroups):
        slab = lg[:, g].astype(F32).reshape(depth, 128).astype(BF16)
        where = g % cgroups
        lcat[g // cgroups, :, where * 128 : (where + 1) * 128] = slab
    left_mask = lg[:, lgroups].astype(F32).reshape(depth, 128)
    right_mask = rg[:, rgroups].astype(F32).reshape(depth, 128)
    counts = dot(right_mask.T.astype(BF16), left_mask.astype(BF16))
    inverse = 1.0 / jnp.maximum(counts, 1.0)
    for i in range(rd):
        rexp[i] = jnp.broadcast_to(inverse[0:cd, i : i + 1], (cd, ch))

    qstep = min(8, pw)

    part = cr // 2

    def to_mirror(step, k, p):
        begin = step * cr + p * part
        src = two.at[pl.ds(begin, part), pl.ds(k * rd, rd)]
        dst = mirror.at[pl.ds((row % fold) * rd + begin, part)]
        return src, dst

    def send_mirror(step, k):
        to_row, to_col = col * fold + k, row // fold
        mine = jnp.logical_and(to_row == row, to_col == col)
        across = to_col // chans != col // chans
        for p in (1, 0):
            src, dst = to_mirror(step, k, p)
            rsem = m_recv.at[row % fold, step, p]
            ssem = m_send.at[k, step, p]

            @pl.when(mine)
            def _():
                pltpu.make_async_copy(src, dst, rsem).start()

            direct = jnp.logical_not(mine)
            if p == 1:
                direct = jnp.logical_and(direct, jnp.logical_not(across))

                @pl.when(across)
                def _():
                    slot, core = to_row // chans, to_row % chans
                    remote(
                        src, relay.at[slot, step], ssem, rl_recv.at[slot, step], row,
                        to_col // chans * chans + core,
                    ).start()

            @pl.when(direct)
            def _():
                remote(src, dst, ssem, rsem, to_row, to_col).start()

    def relayed(m):
        key = m * chans + col % chans
        from_col, to_row, to_col = key // fold, key, row // fold
        active = jnp.logical_and(
            to_col // chans == col // chans, from_col // chans != to_col // chans
        )
        return active, row, to_row, to_col

    def forward(step):
        for m in range(rn // chans):
            active, from_row, to_row, to_col = relayed(m)

            @pl.when(active)
            def _():
                piece = relay.at[m, step]
                pltpu.make_async_copy(piece, piece, rl_recv.at[m, step]).wait()
                begin = (from_row % fold) * rd + step * cr + part
                remote(
                    piece, mirror.at[pl.ds(begin, part)], rl_send.at[m, step],
                    m_recv.at[from_row % fold, step, 1], to_row, to_col,
                ).start()

    lag = min(1, steps)

    def one_step(step, carry):
        lpart = lcat[step]
        for q0 in range(0, pw, qstep):
            z = dot(rq[q0 * cd : (q0 + qstep) * cd, :], lpart).astype(BF16)
            for q in range(qstep):
                for g in range(cgroups):
                    zs[g * cd : (g + 1) * cd, (q0 + q) * 128 : (q0 + q + 1) * 128] = z[
                        q * cd : (q + 1) * cd, g * 128 : (g + 1) * 128
                    ]
        update = dot(zs[...], w4[...])
        for g in range(cgroups):
            for i in range(per):
                at_row = step * cr + g * per + i
                add = update[g * cd : (g + 1) * cd, i * ch : (i + 1) * ch] * rexp[at_row]
                ones[g * per + i] = (pair_ref[at_row].astype(F32) + add).astype(BF16)
        half = max(1, cr // 2)
        for h in range(0, cr, half):
            values = ones[h : h + half].reshape(half * cd, ch).astype(F32)
            centre = jnp.mean(values, axis=-1, keepdims=True)
            shifted = values - centre
            var = jnp.mean(jnp.square(shifted), axis=-1, keepdims=True)
            normed = (shifted * lax.rsqrt(var + epsilon)).astype(BF16)
            gate = dot(normed, wg_ref[...])
            up = dot(normed, wu_ref[...])
            hidden = (gate / (1.0 + jnp.exp(-gate)) * up).astype(BF16)
            result = (values + dot(hidden, wd_ref[...])).astype(BF16)
            two[pl.ds(step * cr + h, half)] = result.reshape(half, cd, ch)
        for k in range(fold):
            send_mirror(step, k)

        @pl.when(step >= lag)
        def _():
            forward(step - lag)

        return carry

    lax.fori_loop(0, steps, one_step, 0)
    for step in range(steps - lag, steps):
        forward(step)

    for step in range(steps):
        for k in range(fold):
            for p in (0, 1):
                piece = mirror.at[pl.ds(k * rd + step * cr + p * part, part)]
                pltpu.make_async_copy(piece, piece, m_recv.at[k, step, p]).wait()
            begin = k * rd + step * cr
            mf[begin * rd : (begin + cr) * rd, :] = (
                mirror[begin : begin + cr].astype(F32).reshape(cr * rd, ch)
            )

    valid_cols = valid_ref[pl.ds(pl.multiple_of(col * cd, 8), cd), :]

    def one_row(i, carry):
        half_sum = (two[i].astype(F32) + mf[pl.ds(i, cd, stride=rd), :]) * 0.5
        sym[i] = half_sum
        masked = half_sum * valid_cols * valid_ref[pl.ds(row * rd + i, 1), :]
        wide[i + 1, :, ch : 2 * ch] = masked.astype(BF16)
        colf[0, pl.ds(i, 1), :] = masked[0:1]
        colf[1, pl.ds(i, 1), :] = masked[cd - 1 : cd]
        return carry

    lax.fori_loop(0, rd, one_row, 0)

    for n, (a, b) in enumerate(AROUND):
        if b == 0:
            hsend[n, 0:cd] = wide[1 if a < 0 else rd, :, ch : 2 * ch]
        elif a == 0:
            hsend[n, 0:rd] = colf[0 if b < 0 else 1].astype(BF16)
        else:
            corner = colf[0 if b < 0 else 1, 0:1] if a < 0 else colf[0 if b < 0 else 1, rd - 1 : rd]
            hsend[n, 0:16] = jnp.broadcast_to(corner, (16, ch)).astype(BF16)

    def there(a, b):
        r, c = row + a, col + b
        return jnp.logical_and(
            jnp.logical_and(r >= 0, r < rn), jnp.logical_and(c >= 0, c < cn)
        )

    def lines(a, b):
        return cd if b == 0 else (rd if a == 0 else 16)

    for n, (a, b) in enumerate(AROUND):

        @pl.when(there(a, b))
        def _():
            size = lines(a, b)
            remote(
                hsend.at[n, pl.ds(0, size)], hrecv.at[n, pl.ds(0, size)], h_send.at[n],
                h_recv.at[n], row + a, col + b,
            ).start()

    for n, (a, b) in enumerate(AROUND):

        @pl.when(there(-a, -b))
        def _():
            piece = hrecv.at[n, pl.ds(0, lines(a, b))]
            pltpu.make_async_copy(piece, piece, h_recv.at[n]).wait()

    slot_of = {direction: n for n, direction in enumerate(AROUND)}
    wide[0, :, ch : 2 * ch] = hrecv[slot_of[(1, 0)], 0:cd]
    wide[rd + 1, :, ch : 2 * ch] = hrecv[slot_of[(-1, 0)], 0:cd]
    colf[0] = hrecv[slot_of[(0, 1)], 0:rd].astype(F32)
    colf[1] = hrecv[slot_of[(0, -1)], 0:rd].astype(F32)
    place = lax.broadcasted_iota(jnp.int32, (cd, ch), 0)

    def widen(i, before, after):
        centre = wide[i, :, ch : 2 * ch].astype(F32)
        wide[i, :, 0:ch] = jnp.where(place == 0, before, pltpu.roll(centre, 1, 0)).astype(BF16)
        wide[i, :, 2 * ch : 3 * ch] = jnp.where(
            place == cd - 1, after, pltpu.roll(centre, cd - 1, 0)
        ).astype(BF16)

    def widen_row(i, carry):
        widen(i + 1, colf[0, pl.ds(i, 1), :], colf[1, pl.ds(i, 1), :])
        return carry

    lax.fori_loop(0, rd, widen_row, 0)
    widen(
        0,
        hrecv[slot_of[(1, 1)], 0:16].astype(F32)[0:1],
        hrecv[slot_of[(1, -1)], 0:16].astype(F32)[0:1],
    )
    widen(
        rd + 1,
        hrecv[slot_of[(-1, 1)], 0:16].astype(F32)[0:1],
        hrecv[slot_of[(-1, -1)], 0:16].astype(F32)[0:1],
    )

    strip = 8

    def conv(n, carry):
        total = sym[pl.ds(n * strip, strip)].reshape(strip * cd, ch)
        for a in range(3):
            window = wide[pl.ds(n * strip + a, strip)].reshape(strip * cd, 3 * ch)
            total = total + dot(window, wk_ref[a])
        out_ref[pl.ds(n * strip, strip)] = total.astype(BF16).reshape(strip, cd, ch)
        return carry

    lax.fori_loop(0, rd // strip, conv, 0)

    for k in range(fold):
        to_row, to_col = col * fold + k, row % cn

        @pl.when(jnp.logical_not(jnp.logical_and(to_row == row, to_col == col)))
        def _():
            pltpu.make_async_copy(lsend.at[k], lsend.at[k], l1_send.at[k]).wait()

        to_row, to_col = col * fold + k, row // fold

        @pl.when(jnp.logical_not(jnp.logical_and(to_row == row, to_col == col)))
        def _():
            for step in range(steps):
                for p in (0, 1):
                    src, _dst = to_mirror(step, k, p)
                    pltpu.make_async_copy(src, src, m_send.at[k, step, p]).wait()

    for m in range(rn // chans):

        @pl.when(relayed(m)[0])
        def _():
            for step in range(steps):
                piece = relay.at[m, step]
                pltpu.make_async_copy(piece, piece, rl_send.at[m, step]).wait()

    for d in range(1, rn):
        pltpu.make_async_copy(rg.at[row], rg.at[row], r_send.at[d - 1]).wait()
    for m in range(fold):
        for d in range(1, cn):
            slot = col + m * cn
            pltpu.make_async_copy(lg.at[slot], lg.at[slot], l2_send.at[m, d - 1]).wait()
    for n, (a, b) in enumerate(AROUND):

        @pl.when(there(a, b))
        def _():
            piece = hsend.at[n, pl.ds(0, lines(a, b))]
            pltpu.make_async_copy(piece, piece, h_send.at[n]).wait()


def on_device(
    mesh_shape,
    pair_input,
    alignment_features,
    alignment_mask,
    token_valid,
    left_weight,
    right_weight,
    output_weight,
    gate_weight,
    up_weight,
    down_weight,
    kernel_weight,
):
    rd, cd, ch = pair_input.shape
    sl, tl, aw = alignment_features.shape
    pw = left_weight.shape[1]
    hid = gate_weight.shape[1]
    rn, chans = mesh_shape["row"], mesh_shape["chan"]
    cn = mesh_shape["col"] * chans
    fold = rn // cn
    per = 128 // pw
    cr = min(16, rd)
    depth = rn * sl
    steps = rd // cr
    tall = max(rd, cd, 16)
    feats = jnp.where((alignment_mask != 0)[:, :, None], alignment_features, 0)
    feats = feats.reshape(sl, tl // per, per * aw).transpose(1, 0, 2).reshape(-1, per * aw)
    valid = jnp.broadcast_to(token_valid.astype(F32)[:, None], (token_valid.shape[0], ch))
    wk = kernel_weight.reshape(3, 3 * ch, ch)
    sizes = (rn, cn, chans, fold, rd, cd, ch, sl, tl, pw, cr)
    dma = pltpu.SemaphoreType.DMA
    vmem = pl.BlockSpec(memory_space=pltpu.VMEM)
    return pl.pallas_call(
        functools.partial(block_kernel, sizes),
        out_shape=jax.ShapeDtypeStruct((rd, cd, ch), BF16),
        in_specs=[vmem] * 11,
        out_specs=vmem,
        scratch_shapes=[
            pltpu.VMEM((fold, rd // per + 1, sl, 128), BF16),
            pltpu.VMEM((rn, rd // per + 1, sl, 128), BF16),
            pltpu.VMEM((rn, cd // per + 1, sl, 128), BF16),
            pltpu.VMEM((cd * pw, depth), F32),
            pltpu.VMEM((pw * cd, depth), BF16),
            pltpu.VMEM((steps, depth, cr * pw), BF16),
            pltpu.VMEM((pw * pw, ch), F32),
            pltpu.VMEM((pw * 128, per * ch), BF16),
            pltpu.VMEM((cr // per * cd, pw * 128), BF16),
            pltpu.VMEM((rd, cd, ch), F32),
            pltpu.VMEM((cr, cd, ch), BF16),
            pltpu.VMEM((rd, cd, ch), BF16),
            pltpu.VMEM((cd, rd, ch), BF16),
            pltpu.VMEM((cd * rd, ch), F32),
            pltpu.VMEM((rd, cd, ch), F32),
            pltpu.VMEM((rd + 2, cd, 3 * ch), BF16),
            pltpu.VMEM((2, rd, ch), F32),
            pltpu.VMEM((8, tall, ch), BF16),
            pltpu.VMEM((8, tall, ch), BF16),
            dma((fold,)),
            dma((fold,)),
            dma((fold, cn - 1)),
            dma((fold, cn - 1)),
            dma((rn - 1,)),
            dma((rn - 1,)),
            dma((fold, steps, 2)),
            dma((fold, steps, 2)),
            pltpu.VMEM((rn // chans, steps, cr // 2, rd, ch), BF16),
            dma((rn // chans, steps)),
            dma((rn // chans, steps)),
            dma((8,)),
            dma((8,)),
        ],
        compiler_params=pltpu.CompilerParams(
            collective_id=0, has_side_effects=True, vmem_limit_bytes=60 * 1024 * 1024
        ),
    )(
        pair_input,
        feats,
        alignment_mask,
        valid,
        left_weight,
        right_weight,
        output_weight,
        gate_weight,
        up_weight,
        down_weight,
        wk,
    )


def solution(mesh):
    placed = (
        P(("groups", "row"), ("col", "chan"), None),
        P("row", ("groups", "col", "chan"), None),
        P("row", ("groups", "col", "chan")),
        P("groups"),
        P(),
        P(),
        P(),
        P(),
        P(),
        P(),
        P(),
    )
    return jax.shard_map(
        functools.partial(on_device, dict(mesh.shape)),
        mesh=mesh,
        in_specs=placed,
        out_specs=P(("groups", "row"), ("col", "chan"), None),
        check_vma=False,
    )
```

```python
import functools

import jax
import jax.numpy as jnp
from jax import lax
from jax.experimental import pallas as pl
from jax.experimental.pallas import tpu as pltpu
from jax.sharding import PartitionSpec as P

epsilon = 1e-05
F32, BF16 = jnp.float32, jnp.bfloat16
MESH = pl.DeviceIdType.MESH
AROUND = [(a, b) for a in (-1, 0, 1) for b in (-1, 0, 1) if (a, b) != (0, 0)]


def dot(a, b):
    return jnp.dot(a, b, preferred_element_type=F32)


def block_kernel(
    sizes,
    feat_ref,
    mask_ref,
    valid_ref,
    wl_ref,
    wr_ref,
    *rest,
):
    far, (out_ref, *rest) = rest[:6], rest[6:]
    near, (w_sem, *rest) = rest[:6], rest[6:]
    pair_ref, wo_ref, wg_ref, wu_ref, wd_ref, wk_ref = near
    (
    proj,
    vrows,
    lsend,
    lg,
    rg,
    rt,
    rq,
    lcat,
    wof,
    w4,
    zs,
    rexp,
    ones,
    two,
    mirror,
    mf,
    sym,
    wide,
    colf,
    hsend,
    hrecv,
    l1_send,
    l1_recv,
    l2_send,
    l2_recv,
    r_send,
    r_recv,
    m_send,
    m_recv,
    relay,
    rl_send,
    rl_recv,
    h_send,
    h_recv,
    ) = rest
    rn, cn, chans, fold, rd, cd, ch, sl, tl, pw, cr = sizes
    row = lax.axis_index("row")
    col = lax.axis_index("col") * chans + lax.axis_index("chan")
    per = 128 // pw
    lgroups, rgroups = rd // per, cd // per
    depth = rn * sl
    steps = rd // cr
    cgroups = cr // per

    def at(r, c):
        return {"row": r, "col": c // chans, "chan": c % chans}

    def remote(src, dst, ssem, rsem, r, c):
        return pltpu.make_async_remote_copy(
            src_ref=src, dst_ref=dst, send_sem=ssem, recv_sem=rsem,
            device_id=at(r, c), device_id_type=MESH,
        )

    order = (1, 0, 2, 3, 4, 5)
    loads = [pltpu.make_async_copy(far[n], near[n], w_sem.at[n]) for n in range(6)]
    for n in order:
        loads[n].start()
    hrecv[...] = jnp.zeros_like(hrecv)
    barrier = pltpu.get_barrier_semaphore()

    def greet(n, carry):
        pl.semaphore_signal(barrier, inc=1, device_id=at(n // cn, n % cn), device_id_type=MESH)
        return carry

    lax.fori_loop(0, rn * cn, greet, 0)

    spread = (
        lax.broadcasted_iota(jnp.int32, (pw, 128), 1) % pw
        == lax.broadcasted_iota(jnp.int32, (pw, 128), 0)
    ).astype(F32).astype(BF16)
    mask = mask_ref[...].astype(F32).astype(BF16)
    spots = tl // per
    token_of = (
        lax.broadcasted_iota(jnp.int32, (tl, spots * 128), 1) // pw
        == lax.broadcasted_iota(jnp.int32, (tl, spots * 128), 0)
    ).astype(F32).astype(BF16)
    wide_mask = dot(mask, token_of)
    feats = feat_ref[...].reshape(sl * tl, feat_ref.shape[2])
    lane_of = lax.broadcasted_iota(jnp.int32, (sl, 128), 1) // pw

    def project(n, w_ref):
        tiled = lax.dot_general(
            w_ref[...], spread, (((0,), (0,)), ((), ())), preferred_element_type=F32
        ).astype(BF16)
        proj[n] = dot(feats, tiled)
        parts = []
        for g in range(spots):
            got = proj[n, pl.ds(g * per, sl, stride=tl), :]
            for t in range(1, per):
                other = proj[n, pl.ds(g * per + t, sl, stride=tl), :]
                got = jnp.where(lane_of == t, other, got)
            parts.append((got * wide_mask[:, g * 128 : (g + 1) * 128]).astype(BF16))
        return parts

    left = project(0, wl_ref)
    right = project(1, wr_ref)
    for k in range(fold):
        for g in range(lgroups):
            lsend[k, g] = left[k * lgroups + g]
        lsend[k, lgroups] = jnp.zeros((sl, 128), BF16)
        lsend[k, lgroups, :, 0:rd] = mask[:, k * rd : (k + 1) * rd]
    for g in range(rgroups):
        rg[row, g] = right[g]
    rg[row, rgroups] = jnp.zeros((sl, 128), BF16)
    rg[row, rgroups, :, 0:tl] = mask

    pl.semaphore_wait(barrier, rn * cn)

    for k in range(fold):
        to_row, to_col = col * fold + k, row % cn
        mine = jnp.logical_and(to_row == row, to_col == col)
        slot = row // cn

        @pl.when(mine)
        def _():
            pltpu.make_async_copy(lsend.at[k], lg.at[row], l1_recv.at[slot]).start()

        @pl.when(jnp.logical_not(mine))
        def _():
            remote(lsend.at[k], lg.at[row], l1_send.at[k], l1_recv.at[slot], to_row, to_col).start()

    def chain(t):
        low, high = jnp.maximum(row - t, 0), jnp.minimum(row + t, rn - 1)
        ups = jnp.logical_and(row - t >= 0, row + 1 < rn)
        downs = jnp.logical_and(row + t < rn, row >= 1)
        return (ups, low, row + 1), (downs, high, row - 1)

    def pass_on(t):
        for way, (go, slot, to_row) in enumerate(chain(t)):

            @pl.when(go)
            def _():
                remote(
                    rg.at[slot], rg.at[slot], r_send.at[way, t], r_recv.at[slot], to_row, col
                ).start()

    pass_on(0)

    tokens = valid_ref.shape[1]
    valid = valid_ref[...].astype(F32)

    def as_rows(first, count):
        hit = lax.broadcasted_iota(jnp.int32, (count, tokens), 1) == first + (
            lax.broadcasted_iota(jnp.int32, (count, tokens), 0)
        )
        chosen = jnp.where(hit, jnp.broadcast_to(valid, (count, tokens)), 0.0).astype(BF16)
        return dot(chosen, jnp.ones((tokens, ch), BF16))

    vrows[0:rd] = as_rows(row * rd, rd)
    valid_cols = as_rows(col * cd, cd)

    loads[1].wait()
    wof[...] = wo_ref[...].astype(F32)
    w4[...] = jnp.zeros_like(w4)
    for q in range(pw):
        part = wof[pl.ds(q, pw, stride=pw), :].astype(BF16)
        for i in range(per):
            w4[q * 128 + i * pw : q * 128 + (i + 1) * pw, i * ch : (i + 1) * ch] = part

    for m in range(fold):
        slot = col + m * cn
        pltpu.make_async_copy(lg.at[slot], lg.at[slot], l1_recv.at[m]).wait()
        for d in range(1, cn):
            remote(
                lg.at[slot], lg.at[slot], l2_send.at[m, d - 1], l2_recv.at[m, d - 1],
                row, (col + d) % cn,
            ).start()

    for t in range(rn - 1):
        if t:
            pass_on(t)
        for there_is, slot in (
            (row - t - 1 >= 0, jnp.maximum(row - t - 1, 0)),
            (row + t + 1 < rn, jnp.minimum(row + t + 1, rn - 1)),
        ):

            @pl.when(there_is)
            def _():
                pltpu.make_async_copy(rg.at[slot], rg.at[slot], r_recv.at[slot]).wait()

    for g in range(rgroups):
        slab = rg[:, g].astype(F32).reshape(depth, 128)
        rt[g * 128 : (g + 1) * 128, :] = slab.T
    for q in range(pw):
        rq[q * cd : (q + 1) * cd, :] = rt[pl.ds(q, cd, stride=pw), :].astype(BF16)

    for m in range(fold):
        for d in range(1, cn):
            slot = (col + cn - d) % cn + m * cn
            pltpu.make_async_copy(lg.at[slot], lg.at[slot], l2_recv.at[m, d - 1]).wait()
    for g in range(lgroups):
        slab = lg[:, g].astype(F32).reshape(depth, 128).astype(BF16)
        where = g % cgroups
        lcat[g // cgroups, :, where * 128 : (where + 1) * 128] = slab
    left_mask = lg[:, lgroups].astype(F32).reshape(depth, 128)
    right_mask = rg[:, rgroups].astype(F32).reshape(depth, 128)
    counts = dot(right_mask.T.astype(BF16), left_mask.astype(BF16))
    inverse = 1.0 / jnp.maximum(counts, 1.0)
    for i in range(rd):
        rexp[i] = jnp.broadcast_to(inverse[0:cd, i : i + 1], (cd, ch))

    for n in (0, 2, 3, 4, 5):
        loads[n].wait()

    qstep = min(8, pw)

    part = cr // 2

    def to_mirror(step, k, p):
        begin = step * cr + p * part
        src = two.at[pl.ds(begin, part), pl.ds(k * rd, rd)]
        dst = mirror.at[pl.ds((row % fold) * rd + begin, part)]
        return src, dst

    def send_mirror(step, k):
        to_row, to_col = col * fold + k, row // fold
        mine = jnp.logical_and(to_row == row, to_col == col)
        across = to_col // chans != col // chans
        for p in (1, 0):
            src, dst = to_mirror(step, k, p)
            rsem = m_recv.at[row % fold, step, p]
            ssem = m_send.at[k, step, p]

            @pl.when(mine)
            def _():
                pltpu.make_async_copy(src, dst, rsem).start()

            direct = jnp.logical_not(mine)
            if p == 1:
                direct = jnp.logical_and(direct, jnp.logical_not(across))

                @pl.when(across)
                def _():
                    slot, core = to_row // chans, to_row % chans
                    remote(
                        src, relay.at[slot, step], ssem, rl_recv.at[slot, step], row,
                        to_col // chans * chans + core,
                    ).start()

            @pl.when(direct)
            def _():
                remote(src, dst, ssem, rsem, to_row, to_col).start()

    def relayed(m):
        key = m * chans + col % chans
        from_col, to_row, to_col = key // fold, key, row // fold
        active = jnp.logical_and(
            to_col // chans == col // chans, from_col // chans != to_col // chans
        )
        return active, row, to_row, to_col

    def forward(step):
        for m in range(rn // chans):
            active, from_row, to_row, to_col = relayed(m)

            @pl.when(active)
            def _():
                piece = relay.at[m, step]
                pltpu.make_async_copy(piece, piece, rl_recv.at[m, step]).wait()
                begin = (from_row % fold) * rd + step * cr + part
                remote(
                    piece, mirror.at[pl.ds(begin, part)], rl_send.at[m, step],
                    m_recv.at[from_row % fold, step, 1], to_row, to_col,
                ).start()

    lag = min(1, steps)

    def one_step(step, carry):
        lpart = lcat[step]
        for q0 in range(0, pw, qstep):
            z = dot(rq[q0 * cd : (q0 + qstep) * cd, :], lpart).astype(BF16)
            for q in range(qstep):
                for g in range(cgroups):
                    zs[g * cd : (g + 1) * cd, (q0 + q) * 128 : (q0 + q + 1) * 128] = z[
                        q * cd : (q + 1) * cd, g * 128 : (g + 1) * 128
                    ]
        update = dot(zs[...], w4[...])
        for g in range(cgroups):
            for i in range(per):
                at_row = step * cr + g * per + i
                add = update[g * cd : (g + 1) * cd, i * ch : (i + 1) * ch] * rexp[at_row]
                ones[g * per + i] = (pair_ref[at_row].astype(F32) + add).astype(BF16)
        half = max(1, cr // 2)
        for h in range(0, cr, half):
            values = ones[h : h + half].reshape(half * cd, ch).astype(F32)
            centre = jnp.mean(values, axis=-1, keepdims=True)
            shifted = values - centre
            var = jnp.mean(jnp.square(shifted), axis=-1, keepdims=True)
            normed = (shifted * lax.rsqrt(var + epsilon)).astype(BF16)
            gate = dot(normed, wg_ref[...])
            up = dot(normed, wu_ref[...])
            hidden = (gate / (1.0 + jnp.exp(-gate)) * up).astype(BF16)
            result = (values + dot(hidden, wd_ref[...])).astype(BF16)
            two[pl.ds(step * cr + h, half)] = result.reshape(half, cd, ch)
        for k in range(fold):
            send_mirror(step, k)

        @pl.when(step >= lag)
        def _():
            forward(step - lag)

        return carry

    lax.fori_loop(0, steps, one_step, 0)
    for step in range(steps - lag, steps):
        forward(step)

    for step in range(steps):
        for k in range(fold):
            begin = k * rd + step * cr
            for p in (0, 1):
                piece = mirror.at[pl.ds(begin + p * part, part)]
                pltpu.make_async_copy(piece, piece, m_recv.at[k, step, p]).wait()
            mf[begin * rd : (begin + cr) * rd, :] = (
                mirror[begin : begin + cr].astype(F32).reshape(cr * rd, ch)
            )
            some_cols = valid_cols[begin : begin + cr]

            def one_row(i, carry):
                other = mf[pl.ds(begin * rd + i, cr, stride=rd), :]
                half_sum = (two[i, begin : begin + cr].astype(F32) + other) * 0.5
                sym[i, begin : begin + cr] = half_sum
                masked = half_sum * some_cols * vrows[pl.ds(i, 1), :]
                wide[i + 1, begin : begin + cr, ch : 2 * ch] = masked.astype(BF16)
                if begin == 0:
                    colf[0, pl.ds(i, 1), :] = masked[0:1]
                if begin + cr == cd:
                    colf[1, pl.ds(i, 1), :] = masked[cr - 1 : cr]
                return carry

            lax.fori_loop(0, rd, one_row, 0, unroll=4)

    for n, (a, b) in enumerate(AROUND):
        if b == 0:
            hsend[n, 0:cd] = wide[1 if a < 0 else rd, :, ch : 2 * ch]
        elif a == 0:
            hsend[n, 0:rd] = colf[0 if b < 0 else 1].astype(BF16)
        else:
            corner = colf[0 if b < 0 else 1, 0:1] if a < 0 else colf[0 if b < 0 else 1, rd - 1 : rd]
            hsend[n, 0:16] = jnp.broadcast_to(corner, (16, ch)).astype(BF16)

    def there(a, b):
        r, c = row + a, col + b
        return jnp.logical_and(
            jnp.logical_and(r >= 0, r < rn), jnp.logical_and(c >= 0, c < cn)
        )

    def lines(a, b):
        return cd if b == 0 else (rd if a == 0 else 16)

    for n, (a, b) in enumerate(AROUND):

        @pl.when(there(a, b))
        def _():
            size = lines(a, b)
            remote(
                hsend.at[n, pl.ds(0, size)], hrecv.at[n, pl.ds(0, size)], h_send.at[n],
                h_recv.at[n], row + a, col + b,
            ).start()

    place = lax.broadcasted_iota(jnp.int32, (cd, ch), 0)

    def widen(i, before, after):
        centre = wide[i, :, ch : 2 * ch].astype(F32)
        wide[i, :, 0:ch] = jnp.where(place == 0, before, pltpu.roll(centre, 1, 0)).astype(BF16)
        wide[i, :, 2 * ch : 3 * ch] = jnp.where(
            place == cd - 1, after, pltpu.roll(centre, cd - 1, 0)
        ).astype(BF16)

    def widen_row(i, carry):
        widen(i + 1, 0.0, 0.0)
        return carry

    lax.fori_loop(0, rd, widen_row, 0, unroll=4)

    for n, (a, b) in enumerate(AROUND):

        @pl.when(there(-a, -b))
        def _():
            piece = hrecv.at[n, pl.ds(0, lines(a, b))]
            pltpu.make_async_copy(piece, piece, h_recv.at[n]).wait()

    slot_of = {direction: n for n, direction in enumerate(AROUND)}
    wide[0, :, ch : 2 * ch] = hrecv[slot_of[(1, 0)], 0:cd]
    wide[rd + 1, :, ch : 2 * ch] = hrecv[slot_of[(-1, 0)], 0:cd]
    colf[0] = hrecv[slot_of[(0, 1)], 0:rd].astype(F32)
    colf[1] = hrecv[slot_of[(0, -1)], 0:rd].astype(F32)
    edge = lax.broadcasted_iota(jnp.int32, (16, ch), 0)

    def patch_row(i, carry):
        first = wide[i + 1, 0:16, 0:ch].astype(F32)
        wide[i + 1, 0:16, 0:ch] = jnp.where(
            edge == 0, colf[0, pl.ds(i, 1), :], first
        ).astype(BF16)
        last = wide[i + 1, cd - 16 : cd, 2 * ch : 3 * ch].astype(F32)
        wide[i + 1, cd - 16 : cd, 2 * ch : 3 * ch] = jnp.where(
            edge == 15, colf[1, pl.ds(i, 1), :], last
        ).astype(BF16)
        return carry

    lax.fori_loop(0, rd, patch_row, 0, unroll=4)
    widen(
        0,
        hrecv[slot_of[(1, 1)], 0:16].astype(F32)[0:1],
        hrecv[slot_of[(1, -1)], 0:16].astype(F32)[0:1],
    )
    widen(
        rd + 1,
        hrecv[slot_of[(-1, 1)], 0:16].astype(F32)[0:1],
        hrecv[slot_of[(-1, -1)], 0:16].astype(F32)[0:1],
    )

    strip = 8

    def conv(n, carry):
        total = sym[pl.ds(n * strip, strip)].reshape(strip * cd, ch)
        for a in range(3):
            window = wide[pl.ds(n * strip + a, strip)].reshape(strip * cd, 3 * ch)
            total = total + dot(window, wk_ref[a])
        out_ref[pl.ds(n * strip, strip)] = total.astype(BF16).reshape(strip, cd, ch)
        return carry

    lax.fori_loop(0, rd // strip, conv, 0)

    for k in range(fold):
        to_row, to_col = col * fold + k, row % cn

        @pl.when(jnp.logical_not(jnp.logical_and(to_row == row, to_col == col)))
        def _():
            pltpu.make_async_copy(lsend.at[k], lsend.at[k], l1_send.at[k]).wait()

        to_row, to_col = col * fold + k, row // fold

        @pl.when(jnp.logical_not(jnp.logical_and(to_row == row, to_col == col)))
        def _():
            for step in range(steps):
                for p in (0, 1):
                    src, _dst = to_mirror(step, k, p)
                    pltpu.make_async_copy(src, src, m_send.at[k, step, p]).wait()

    for m in range(rn // chans):

        @pl.when(relayed(m)[0])
        def _():
            for step in range(steps):
                piece = relay.at[m, step]
                pltpu.make_async_copy(piece, piece, rl_send.at[m, step]).wait()

    for t in range(rn - 1):
        for way, (go, slot, _to_row) in enumerate(chain(t)):

            @pl.when(go)
            def _():
                pltpu.make_async_copy(rg.at[slot], rg.at[slot], r_send.at[way, t]).wait()

    for m in range(fold):
        for d in range(1, cn):
            slot = col + m * cn
            pltpu.make_async_copy(lg.at[slot], lg.at[slot], l2_send.at[m, d - 1]).wait()
    for n, (a, b) in enumerate(AROUND):

        @pl.when(there(a, b))
        def _():
            piece = hsend.at[n, pl.ds(0, lines(a, b))]
            pltpu.make_async_copy(piece, piece, h_send.at[n]).wait()


def on_device(
    mesh_shape,
    pair_input,
    alignment_features,
    alignment_mask,
    token_valid,
    left_weight,
    right_weight,
    output_weight,
    gate_weight,
    up_weight,
    down_weight,
    kernel_weight,
):
    rd, cd, ch = pair_input.shape
    sl, tl, aw = alignment_features.shape
    pw = left_weight.shape[1]
    hid = gate_weight.shape[1]
    rn, chans = mesh_shape["row"], mesh_shape["chan"]
    cn = mesh_shape["col"] * chans
    fold = rn // cn
    per = 128 // pw
    cr = min(16, rd)
    depth = rn * sl
    steps = rd // cr
    tall = max(rd, cd, 16)
    wk = kernel_weight.reshape(3, 3 * ch, ch)
    sizes = (rn, cn, chans, fold, rd, cd, ch, sl, tl, pw, cr)
    large = (pair_input, output_weight, gate_weight, up_weight, down_weight, wk)
    dma = pltpu.SemaphoreType.DMA
    vmem = pl.BlockSpec(memory_space=pltpu.VMEM)
    return pl.pallas_call(
        functools.partial(block_kernel, sizes),
        out_shape=jax.ShapeDtypeStruct((rd, cd, ch), BF16),
        in_specs=[vmem] * 5 + [pl.BlockSpec(memory_space=pl.ANY)] * 6,
        out_specs=vmem,
        scratch_shapes=[
            *[pltpu.VMEM(value.shape, value.dtype) for value in large],
            dma((6,)),
            pltpu.VMEM((2, sl * tl, 128), F32),
            pltpu.VMEM((tall, ch), F32),
            pltpu.VMEM((fold, rd // per + 1, sl, 128), BF16),
            pltpu.VMEM((rn, rd // per + 1, sl, 128), BF16),
            pltpu.VMEM((rn, cd // per + 1, sl, 128), BF16),
            pltpu.VMEM((cd * pw, depth), F32),
            pltpu.VMEM((pw * cd, depth), BF16),
            pltpu.VMEM((steps, depth, cr * pw), BF16),
            pltpu.VMEM((pw * pw, ch), F32),
            pltpu.VMEM((pw * 128, per * ch), BF16),
            pltpu.VMEM((cr // per * cd, pw * 128), BF16),
            pltpu.VMEM((rd, cd, ch), F32),
            pltpu.VMEM((cr, cd, ch), BF16),
            pltpu.VMEM((rd, cd, ch), BF16),
            pltpu.VMEM((cd, rd, ch), BF16),
            pltpu.VMEM((cd * rd, ch), F32),
            pltpu.VMEM((rd, cd, ch), F32),
            pltpu.VMEM((rd + 2, cd, 3 * ch), BF16),
            pltpu.VMEM((2, rd, ch), F32),
            pltpu.VMEM((8, tall, ch), BF16),
            pltpu.VMEM((8, tall, ch), BF16),
            dma((fold,)),
            dma((fold,)),
            dma((fold, cn - 1)),
            dma((fold, cn - 1)),
            dma((2, rn - 1)),
            dma((rn,)),
            dma((fold, steps, 2)),
            dma((fold, steps, 2)),
            pltpu.VMEM((rn // chans, steps, cr // 2, rd, ch), BF16),
            dma((rn // chans, steps)),
            dma((rn // chans, steps)),
            dma((8,)),
            dma((8,)),
        ],
        compiler_params=pltpu.CompilerParams(
            collective_id=0, has_side_effects=True, vmem_limit_bytes=60 * 1024 * 1024
        ),
    )(
        alignment_features,
        alignment_mask,
        token_valid.reshape(1, -1),
        left_weight.T,
        right_weight.T,
        *large,
    )


def solution(mesh):
    placed = (
        P(("groups", "row"), ("col", "chan"), None),
        P("row", ("groups", "col", "chan"), None),
        P("row", ("groups", "col", "chan")),
        P("groups"),
        P(),
        P(),
        P(),
        P(),
        P(),
        P(),
        P(),
    )
    return jax.shard_map(
        functools.partial(on_device, dict(mesh.shape)),
        mesh=mesh,
        in_specs=placed,
        out_specs=P(("groups", "row"), ("col", "chan"), None),
        check_vma=False,
    )
```

```python
import functools

import jax
import jax.numpy as jnp
from jax import lax
from jax.experimental import pallas as pl
from jax.experimental.pallas import tpu as pltpu
from jax.sharding import PartitionSpec as P

epsilon = 1e-05
F32, BF16 = jnp.float32, jnp.bfloat16
MESH = pl.DeviceIdType.MESH
AROUND = [(a, b) for a in (-1, 0, 1) for b in (-1, 0, 1) if (a, b) != (0, 0)]


def dot(a, b):
    return jnp.dot(a, b, preferred_element_type=F32)


def block_kernel(
    sizes,
    feat_ref,
    mask_ref,
    valid_ref,
    wl_ref,
    wr_ref,
    *rest,
):
    far, (out_ref, *rest) = rest[:6], rest[6:]
    near, (w_sem, *rest) = rest[:6], rest[6:]
    pair_ref, wo_ref, wg_ref, wu_ref, wd_ref, wk_ref = near
    (
    proj,
    vrows,
    lsend,
    lg,
    rg,
    rt,
    rq,
    lcat,
    wof,
    w4,
    zs,
    rexp,
    ones,
    two,
    mirror,
    mf,
    sym,
    wide,
    colf,
    hsend,
    hrecv,
    l1_send,
    l1_recv,
    l2_send,
    l2_recv,
    r_send,
    r_recv,
    m_send,
    m_recv,
    relay,
    rl_send,
    rl_recv,
    h_send,
    h_recv,
    ) = rest
    rn, cn, chans, fold, rd, cd, ch, sl, tl, pw, cr = sizes
    row = lax.axis_index("row")
    col = lax.axis_index("col") * chans + lax.axis_index("chan")
    per = 128 // pw
    lgroups, rgroups = rd // per, cd // per
    depth = rn * sl
    steps = rd // cr
    cgroups = cr // per

    def at(r, c):
        return {"row": r, "col": c // chans, "chan": c % chans}

    def remote(src, dst, ssem, rsem, r, c):
        return pltpu.make_async_remote_copy(
            src_ref=src, dst_ref=dst, send_sem=ssem, recv_sem=rsem,
            device_id=at(r, c), device_id_type=MESH,
        )

    order = (1, 0, 2, 3, 4, 5)
    loads = [pltpu.make_async_copy(far[n], near[n], w_sem.at[n]) for n in range(6)]
    for n in order:
        loads[n].start()
    hrecv[...] = jnp.zeros_like(hrecv)
    barrier = pltpu.get_barrier_semaphore()

    def greet(n, carry):
        pl.semaphore_signal(barrier, inc=1, device_id=at(n // cn, n % cn), device_id_type=MESH)
        return carry

    lax.fori_loop(0, rn * cn, greet, 0)

    spread = (
        lax.broadcasted_iota(jnp.int32, (pw, 128), 1) % pw
        == lax.broadcasted_iota(jnp.int32, (pw, 128), 0)
    ).astype(F32).astype(BF16)
    mask = mask_ref[...].astype(F32).astype(BF16)
    spots = tl // per
    token_of = (
        lax.broadcasted_iota(jnp.int32, (tl, spots * 128), 1) // pw
        == lax.broadcasted_iota(jnp.int32, (tl, spots * 128), 0)
    ).astype(F32).astype(BF16)
    wide_mask = dot(mask, token_of)
    feats = feat_ref[...].reshape(sl * tl, feat_ref.shape[2])
    lane_of = lax.broadcasted_iota(jnp.int32, (sl, 128), 1) // pw

    def project(n, w_ref):
        tiled = lax.dot_general(
            w_ref[...], spread, (((0,), (0,)), ((), ())), preferred_element_type=F32
        ).astype(BF16)
        proj[n] = dot(feats, tiled)
        parts = []
        for g in range(spots):
            got = proj[n, pl.ds(g * per, sl, stride=tl), :]
            for t in range(1, per):
                other = proj[n, pl.ds(g * per + t, sl, stride=tl), :]
                got = jnp.where(lane_of == t, other, got)
            parts.append((got * wide_mask[:, g * 128 : (g + 1) * 128]).astype(BF16))
        return parts

    left = project(0, wl_ref)
    right = project(1, wr_ref)
    for k in range(fold):
        for g in range(lgroups):
            lsend[k, g] = left[k * lgroups + g]
        lsend[k, lgroups] = jnp.zeros((sl, 128), BF16)
        lsend[k, lgroups, :, 0:rd] = mask[:, k * rd : (k + 1) * rd]
    for g in range(rgroups):
        rg[row, g] = right[g]
    rg[row, rgroups] = jnp.zeros((sl, 128), BF16)
    rg[row, rgroups, :, 0:tl] = mask

    pl.semaphore_wait(barrier, rn * cn)

    for k in range(fold):
        to_row, to_col = col * fold + k, row % cn
        mine = jnp.logical_and(to_row == row, to_col == col)
        slot = row // cn

        @pl.when(mine)
        def _():
            pltpu.make_async_copy(lsend.at[k], lg.at[row], l1_recv.at[slot]).start()

        @pl.when(jnp.logical_not(mine))
        def _():
            remote(lsend.at[k], lg.at[row], l1_send.at[k], l1_recv.at[slot], to_row, to_col).start()

    def chain(t):
        low, high = jnp.maximum(row - t, 0), jnp.minimum(row + t, rn - 1)
        ups = jnp.logical_and(row - t >= 0, row + 1 < rn)
        downs = jnp.logical_and(row + t < rn, row >= 1)
        return (ups, low, row + 1), (downs, high, row - 1)

    cut = rgroups // 2
    pieces = (pl.ds(0, cut), pl.ds(cut, rgroups + 1 - cut))

    def pass_on(t):
        for way, (go, slot, to_row) in enumerate(chain(t)):

            @pl.when(go)
            def _():
                for e, piece in enumerate(pieces):
                    part_of = rg.at[slot, piece]
                    remote(
                        part_of, part_of, r_send.at[way, t, e], r_recv.at[slot, e], to_row, col
                    ).start()

    pass_on(0)

    tokens = valid_ref.shape[1]
    valid = valid_ref[...].astype(F32)

    def as_rows(first, count):
        hit = lax.broadcasted_iota(jnp.int32, (count, tokens), 1) == first + (
            lax.broadcasted_iota(jnp.int32, (count, tokens), 0)
        )
        chosen = jnp.where(hit, jnp.broadcast_to(valid, (count, tokens)), 0.0).astype(BF16)
        return dot(chosen, jnp.ones((tokens, ch), BF16))

    vrows[0:rd] = as_rows(row * rd, rd)
    valid_cols = as_rows(col * cd, cd)

    loads[1].wait()
    wof[...] = wo_ref[...].astype(F32)
    w4[...] = jnp.zeros_like(w4)
    for q in range(pw):
        part = wof[pl.ds(q, pw, stride=pw), :].astype(BF16)
        for i in range(per):
            w4[q * 128 + i * pw : q * 128 + (i + 1) * pw, i * ch : (i + 1) * ch] = part

    for m in range(fold):
        slot = col + m * cn
        pltpu.make_async_copy(lg.at[slot], lg.at[slot], l1_recv.at[m]).wait()
        for d in range(1, cn):
            remote(
                lg.at[slot], lg.at[slot], l2_send.at[m, d - 1], l2_recv.at[m, d - 1],
                row, (col + d) % cn,
            ).start()

    for t in range(rn - 1):
        for e, piece in enumerate(pieces):
            for way, (there_is, slot) in enumerate((
                (row - t - 1 >= 0, jnp.maximum(row - t - 1, 0)),
                (row + t + 1 < rn, jnp.minimum(row + t + 1, rn - 1)),
            )):

                @pl.when(there_is)
                def _():
                    part_of = rg.at[slot, piece]
                    pltpu.make_async_copy(part_of, part_of, r_recv.at[slot, e]).wait()

                if t + 1 < rn - 1:
                    go, _slot, to_row = chain(t + 1)[way]

                    @pl.when(go)
                    def _():
                        part_of = rg.at[slot, piece]
                        remote(
                            part_of, part_of, r_send.at[way, t + 1, e], r_recv.at[slot, e],
                            to_row, col,
                        ).start()

    for g in range(rgroups):
        slab = rg[:, g].astype(F32).reshape(depth, 128)
        rt[g * 128 : (g + 1) * 128, :] = slab.T
    for q in range(pw):
        rq[q * cd : (q + 1) * cd, :] = rt[pl.ds(q, cd, stride=pw), :].astype(BF16)

    for m in range(fold):
        for d in range(1, cn):
            slot = (col + cn - d) % cn + m * cn
            pltpu.make_async_copy(lg.at[slot], lg.at[slot], l2_recv.at[m, d - 1]).wait()
    for g in range(lgroups):
        slab = lg[:, g].astype(F32).reshape(depth, 128).astype(BF16)
        where = g % cgroups
        lcat[g // cgroups, :, where * 128 : (where + 1) * 128] = slab
    left_mask = lg[:, lgroups].astype(F32).reshape(depth, 128)
    right_mask = rg[:, rgroups].astype(F32).reshape(depth, 128)
    counts = dot(right_mask.T.astype(BF16), left_mask.astype(BF16))
    inverse = 1.0 / jnp.maximum(counts, 1.0)
    for i in range(rd):
        rexp[i] = jnp.broadcast_to(inverse[0:cd, i : i + 1], (cd, ch))

    for n in (0, 2, 3, 4, 5):
        loads[n].wait()

    qstep = min(8, pw)

    part = cr // 2

    def to_mirror(step, k, p):
        begin = step * cr + p * part
        src = two.at[pl.ds(begin, part), pl.ds(k * rd, rd)]
        dst = mirror.at[pl.ds((row % fold) * rd + begin, part)]
        return src, dst

    def send_mirror(step, k, p):
        to_row, to_col = col * fold + k, row // fold
        mine = jnp.logical_and(to_row == row, to_col == col)
        across = to_col // chans != col // chans
        src, dst = to_mirror(step, k, p)
        rsem = m_recv.at[row % fold, step, p]
        ssem = m_send.at[k, step, p]

        @pl.when(mine)
        def _():
            pltpu.make_async_copy(src, dst, rsem).start()

        direct = jnp.logical_not(mine)
        if p == 1:
            direct = jnp.logical_and(direct, jnp.logical_not(across))

            @pl.when(across)
            def _():
                slot, core = to_row // chans, to_row % chans
                remote(
                    src, relay.at[slot, step], ssem, rl_recv.at[slot, step], row,
                    to_col // chans * chans + core,
                ).start()

        @pl.when(direct)
        def _():
            remote(src, dst, ssem, rsem, to_row, to_col).start()

    def relayed(m):
        key = m * chans + col % chans
        from_col, to_row, to_col = key // fold, key, row // fold
        active = jnp.logical_and(
            to_col // chans == col // chans, from_col // chans != to_col // chans
        )
        return active, row, to_row, to_col

    def forward(step):
        for m in range(rn // chans):
            active, from_row, to_row, to_col = relayed(m)

            @pl.when(active)
            def _():
                piece = relay.at[m, step]
                pltpu.make_async_copy(piece, piece, rl_recv.at[m, step]).wait()
                begin = (from_row % fold) * rd + step * cr + part
                remote(
                    piece, mirror.at[pl.ds(begin, part)], rl_send.at[m, step],
                    m_recv.at[from_row % fold, step, 1], to_row, to_col,
                ).start()

    lag = min(1, steps)

    def one_step(step, carry):
        lpart = lcat[step]
        for q0 in range(0, pw, qstep):
            z = dot(rq[q0 * cd : (q0 + qstep) * cd, :], lpart).astype(BF16)
            for q in range(qstep):
                for g in range(cgroups):
                    zs[g * cd : (g + 1) * cd, (q0 + q) * 128 : (q0 + q + 1) * 128] = z[
                        q * cd : (q + 1) * cd, g * 128 : (g + 1) * 128
                    ]
        update = dot(zs[...], w4[...])
        for g in range(cgroups):
            for i in range(per):
                at_row = step * cr + g * per + i
                add = update[g * cd : (g + 1) * cd, i * ch : (i + 1) * ch] * rexp[at_row]
                ones[g * per + i] = (pair_ref[at_row].astype(F32) + add).astype(BF16)
        for p in (1, 0):
            values = ones[p * part : (p + 1) * part].reshape(part * cd, ch).astype(F32)
            centre = jnp.mean(values, axis=-1, keepdims=True)
            shifted = values - centre
            var = jnp.mean(jnp.square(shifted), axis=-1, keepdims=True)
            normed = (shifted * lax.rsqrt(var + epsilon)).astype(BF16)
            gate = dot(normed, wg_ref[...])
            up = dot(normed, wu_ref[...])
            hidden = (gate / (1.0 + jnp.exp(-gate)) * up).astype(BF16)
            result = (values + dot(hidden, wd_ref[...])).astype(BF16)
            two[pl.ds(step * cr + p * part, part)] = result.reshape(part, cd, ch)
            for k in range(fold):
                send_mirror(step, k, p)
            if p == 1:

                @pl.when(step >= lag)
                def _():
                    forward(step - lag)

        return carry

    lax.fori_loop(0, steps, one_step, 0)
    for step in range(steps - lag, steps):
        forward(step)

    for step in range(steps):
        for k in range(fold):
            begin = k * rd + step * cr
            for p in (0, 1):
                piece = mirror.at[pl.ds(begin + p * part, part)]
                pltpu.make_async_copy(piece, piece, m_recv.at[k, step, p]).wait()
            mf[begin * rd : (begin + cr) * rd, :] = (
                mirror[begin : begin + cr].astype(F32).reshape(cr * rd, ch)
            )
            some_cols = valid_cols[begin : begin + cr]

            def one_row(i, carry):
                other = mf[pl.ds(begin * rd + i, cr, stride=rd), :]
                half_sum = (two[i, begin : begin + cr].astype(F32) + other) * 0.5
                sym[i, begin : begin + cr] = half_sum
                masked = half_sum * some_cols * vrows[pl.ds(i, 1), :]
                wide[i + 1, begin : begin + cr, ch : 2 * ch] = masked.astype(BF16)
                if begin == 0:
                    colf[0, pl.ds(i, 1), :] = masked[0:1]
                if begin + cr == cd:
                    colf[1, pl.ds(i, 1), :] = masked[cr - 1 : cr]
                return carry

            lax.fori_loop(0, rd, one_row, 0, unroll=4)

    for n, (a, b) in enumerate(AROUND):
        if b == 0:
            hsend[n, 0:cd] = wide[1 if a < 0 else rd, :, ch : 2 * ch]
        elif a == 0:
            hsend[n, 0:rd] = colf[0 if b < 0 else 1].astype(BF16)
        else:
            corner = colf[0 if b < 0 else 1, 0:1] if a < 0 else colf[0 if b < 0 else 1, rd - 1 : rd]
            hsend[n, 0:16] = jnp.broadcast_to(corner, (16, ch)).astype(BF16)

    def there(a, b):
        r, c = row + a, col + b
        return jnp.logical_and(
            jnp.logical_and(r >= 0, r < rn), jnp.logical_and(c >= 0, c < cn)
        )

    def lines(a, b):
        return cd if b == 0 else (rd if a == 0 else 16)

    for n, (a, b) in enumerate(AROUND):

        @pl.when(there(a, b))
        def _():
            size = lines(a, b)
            remote(
                hsend.at[n, pl.ds(0, size)], hrecv.at[n, pl.ds(0, size)], h_send.at[n],
                h_recv.at[n], row + a, col + b,
            ).start()

    place = lax.broadcasted_iota(jnp.int32, (cd, ch), 0)

    def widen(i, before, after):
        centre = wide[i, :, ch : 2 * ch].astype(F32)
        wide[i, :, 0:ch] = jnp.where(place == 0, before, pltpu.roll(centre, 1, 0)).astype(BF16)
        wide[i, :, 2 * ch : 3 * ch] = jnp.where(
            place == cd - 1, after, pltpu.roll(centre, cd - 1, 0)
        ).astype(BF16)

    def widen_row(i, carry):
        widen(i + 1, 0.0, 0.0)
        return carry

    lax.fori_loop(0, rd, widen_row, 0, unroll=4)

    for n, (a, b) in enumerate(AROUND):

        @pl.when(there(-a, -b))
        def _():
            piece = hrecv.at[n, pl.ds(0, lines(a, b))]
            pltpu.make_async_copy(piece, piece, h_recv.at[n]).wait()

    slot_of = {direction: n for n, direction in enumerate(AROUND)}
    wide[0, :, ch : 2 * ch] = hrecv[slot_of[(1, 0)], 0:cd]
    wide[rd + 1, :, ch : 2 * ch] = hrecv[slot_of[(-1, 0)], 0:cd]
    colf[0] = hrecv[slot_of[(0, 1)], 0:rd].astype(F32)
    colf[1] = hrecv[slot_of[(0, -1)], 0:rd].astype(F32)
    edge = lax.broadcasted_iota(jnp.int32, (16, ch), 0)

    def patch_row(i, carry):
        first = wide[i + 1, 0:16, 0:ch].astype(F32)
        wide[i + 1, 0:16, 0:ch] = jnp.where(
            edge == 0, colf[0, pl.ds(i, 1), :], first
        ).astype(BF16)
        last = wide[i + 1, cd - 16 : cd, 2 * ch : 3 * ch].astype(F32)
        wide[i + 1, cd - 16 : cd, 2 * ch : 3 * ch] = jnp.where(
            edge == 15, colf[1, pl.ds(i, 1), :], last
        ).astype(BF16)
        return carry

    lax.fori_loop(0, rd, patch_row, 0, unroll=4)
    widen(
        0,
        hrecv[slot_of[(1, 1)], 0:16].astype(F32)[0:1],
        hrecv[slot_of[(1, -1)], 0:16].astype(F32)[0:1],
    )
    widen(
        rd + 1,
        hrecv[slot_of[(-1, 1)], 0:16].astype(F32)[0:1],
        hrecv[slot_of[(-1, -1)], 0:16].astype(F32)[0:1],
    )

    strip = 8

    def conv(n, carry):
        total = sym[pl.ds(n * strip, strip)].reshape(strip * cd, ch)
        for a in range(3):
            window = wide[pl.ds(n * strip + a, strip)].reshape(strip * cd, 3 * ch)
            total = total + dot(window, wk_ref[a])
        out_ref[pl.ds(n * strip, strip)] = total.astype(BF16).reshape(strip, cd, ch)
        return carry

    lax.fori_loop(0, rd // strip, conv, 0)

    for k in range(fold):
        to_row, to_col = col * fold + k, row % cn

        @pl.when(jnp.logical_not(jnp.logical_and(to_row == row, to_col == col)))
        def _():
            pltpu.make_async_copy(lsend.at[k], lsend.at[k], l1_send.at[k]).wait()

        to_row, to_col = col * fold + k, row // fold

        @pl.when(jnp.logical_not(jnp.logical_and(to_row == row, to_col == col)))
        def _():
            for step in range(steps):
                for p in (0, 1):
                    src, _dst = to_mirror(step, k, p)
                    pltpu.make_async_copy(src, src, m_send.at[k, step, p]).wait()

    for m in range(rn // chans):

        @pl.when(relayed(m)[0])
        def _():
            for step in range(steps):
                piece = relay.at[m, step]
                pltpu.make_async_copy(piece, piece, rl_send.at[m, step]).wait()

    for t in range(rn - 1):
        for way, (go, slot, _to_row) in enumerate(chain(t)):

            @pl.when(go)
            def _():
                for e, piece in enumerate(pieces):
                    part_of = rg.at[slot, piece]
                    pltpu.make_async_copy(part_of, part_of, r_send.at[way, t, e]).wait()

    for m in range(fold):
        for d in range(1, cn):
            slot = col + m * cn
            pltpu.make_async_copy(lg.at[slot], lg.at[slot], l2_send.at[m, d - 1]).wait()
    for n, (a, b) in enumerate(AROUND):

        @pl.when(there(a, b))
        def _():
            piece = hsend.at[n, pl.ds(0, lines(a, b))]
            pltpu.make_async_copy(piece, piece, h_send.at[n]).wait()


def on_device(
    mesh_shape,
    pair_input,
    alignment_features,
    alignment_mask,
    token_valid,
    left_weight,
    right_weight,
    output_weight,
    gate_weight,
    up_weight,
    down_weight,
    kernel_weight,
):
    rd, cd, ch = pair_input.shape
    sl, tl, aw = alignment_features.shape
    pw = left_weight.shape[1]
    hid = gate_weight.shape[1]
    rn, chans = mesh_shape["row"], mesh_shape["chan"]
    cn = mesh_shape["col"] * chans
    fold = rn // cn
    per = 128 // pw
    cr = min(16, rd)
    depth = rn * sl
    steps = rd // cr
    tall = max(rd, cd, 16)
    wk = kernel_weight.reshape(3, 3 * ch, ch)
    sizes = (rn, cn, chans, fold, rd, cd, ch, sl, tl, pw, cr)
    large = (pair_input, output_weight, gate_weight, up_weight, down_weight, wk)
    dma = pltpu.SemaphoreType.DMA
    vmem = pl.BlockSpec(memory_space=pltpu.VMEM)
    return pl.pallas_call(
        functools.partial(block_kernel, sizes),
        out_shape=jax.ShapeDtypeStruct((rd, cd, ch), BF16),
        in_specs=[vmem] * 5 + [pl.BlockSpec(memory_space=pl.ANY)] * 6,
        out_specs=vmem,
        scratch_shapes=[
            *[pltpu.VMEM(value.shape, value.dtype) for value in large],
            dma((6,)),
            pltpu.VMEM((2, sl * tl, 128), F32),
            pltpu.VMEM((tall, ch), F32),
            pltpu.VMEM((fold, rd // per + 1, sl, 128), BF16),
            pltpu.VMEM((rn, rd // per + 1, sl, 128), BF16),
            pltpu.VMEM((rn, cd // per + 1, sl, 128), BF16),
            pltpu.VMEM((cd * pw, depth), F32),
            pltpu.VMEM((pw * cd, depth), BF16),
            pltpu.VMEM((steps, depth, cr * pw), BF16),
            pltpu.VMEM((pw * pw, ch), F32),
            pltpu.VMEM((pw * 128, per * ch), BF16),
            pltpu.VMEM((cr // per * cd, pw * 128), BF16),
            pltpu.VMEM((rd, cd, ch), F32),
            pltpu.VMEM((cr, cd, ch), BF16),
            pltpu.VMEM((rd, cd, ch), BF16),
            pltpu.VMEM((cd, rd, ch), BF16),
            pltpu.VMEM((cd * rd, ch), F32),
            pltpu.VMEM((rd, cd, ch), F32),
            pltpu.VMEM((rd + 2, cd, 3 * ch), BF16),
            pltpu.VMEM((2, rd, ch), F32),
            pltpu.VMEM((8, tall, ch), BF16),
            pltpu.VMEM((8, tall, ch), BF16),
            dma((fold,)),
            dma((fold,)),
            dma((fold, cn - 1)),
            dma((fold, cn - 1)),
            dma((2, rn - 1, 2)),
            dma((rn, 2)),
            dma((fold, steps, 2)),
            dma((fold, steps, 2)),
            pltpu.VMEM((rn // chans, steps, cr // 2, rd, ch), BF16),
            dma((rn // chans, steps)),
            dma((rn // chans, steps)),
            dma((8,)),
            dma((8,)),
        ],
        compiler_params=pltpu.CompilerParams(
            collective_id=0, has_side_effects=True, vmem_limit_bytes=60 * 1024 * 1024
        ),
    )(
        alignment_features,
        alignment_mask,
        token_valid.reshape(1, -1),
        left_weight.T,
        right_weight.T,
        *large,
    )


def solution(mesh):
    placed = (
        P(("groups", "row"), ("col", "chan"), None),
        P("row", ("groups", "col", "chan"), None),
        P("row", ("groups", "col", "chan")),
        P("groups"),
        P(),
        P(),
        P(),
        P(),
        P(),
        P(),
        P(),
    )
    return jax.shard_map(
        functools.partial(on_device, dict(mesh.shape)),
        mesh=mesh,
        in_specs=placed,
        out_specs=P(("groups", "row"), ("col", "chan"), None),
        check_vma=False,
    )
```

```python
import functools

import jax
import jax.numpy as jnp
from jax import lax
from jax.experimental import pallas as pl
from jax.experimental.pallas import tpu as pltpu
from jax.sharding import PartitionSpec as P

epsilon = 1e-05
F32, BF16 = jnp.float32, jnp.bfloat16
MESH = pl.DeviceIdType.MESH
AROUND = [(a, b) for a in (-1, 0, 1) for b in (-1, 0, 1) if (a, b) != (0, 0)]


def dot(a, b):
    return jnp.dot(a, b, preferred_element_type=F32)


def block_kernel(
    sizes,
    feat_ref,
    mask_ref,
    valid_ref,
    wl_ref,
    wr_ref,
    *rest,
):
    far, (out_ref, *rest) = rest[:6], rest[6:]
    near, (w_sem, *rest) = rest[:6], rest[6:]
    pair_ref, wo_ref, wg_ref, wu_ref, wd_ref, wk_ref = near
    (
    proj,
    vrows,
    lsend,
    lg,
    rg,
    rt,
    rq,
    lcat,
    wof,
    w4,
    zs,
    rexp,
    ones,
    two,
    mirror,
    mf,
    sym,
    wide,
    colf,
    hsend,
    hrecv,
    l1_send,
    l1_recv,
    l2_send,
    l2_recv,
    r_send,
    r_recv,
    m_send,
    m_recv,
    relay,
    rl_send,
    rl_recv,
    h_send,
    h_recv,
    ) = rest
    rn, cn, chans, fold, rd, cd, ch, sl, tl, pw, cr = sizes
    row = lax.axis_index("row")
    col = lax.axis_index("col") * chans + lax.axis_index("chan")
    per = 128 // pw
    lgroups, rgroups = rd // per, cd // per
    depth = rn * sl
    steps = rd // cr
    cgroups = cr // per

    def at(r, c):
        return {"row": r, "col": c // chans, "chan": c % chans}

    def remote(src, dst, ssem, rsem, r, c):
        return pltpu.make_async_remote_copy(
            src_ref=src, dst_ref=dst, send_sem=ssem, recv_sem=rsem,
            device_id=at(r, c), device_id_type=MESH,
        )

    order = (1, 0, 2, 3, 4, 5)
    loads = [pltpu.make_async_copy(far[n], near[n], w_sem.at[n]) for n in range(6)]
    for n in order:
        loads[n].start()
    hrecv[...] = jnp.zeros_like(hrecv)
    barrier = pltpu.get_barrier_semaphore()

    def greet(n, carry):
        pl.semaphore_signal(barrier, inc=1, device_id=at(n // cn, n % cn), device_id_type=MESH)
        return carry

    lax.fori_loop(0, rn * cn, greet, 0)

    spread = (
        lax.broadcasted_iota(jnp.int32, (pw, 128), 1) % pw
        == lax.broadcasted_iota(jnp.int32, (pw, 128), 0)
    ).astype(F32).astype(BF16)
    mask = mask_ref[...].astype(F32).astype(BF16)
    spots = tl // per
    token_of = (
        lax.broadcasted_iota(jnp.int32, (tl, spots * 128), 1) // pw
        == lax.broadcasted_iota(jnp.int32, (tl, spots * 128), 0)
    ).astype(F32).astype(BF16)
    wide_mask = dot(mask, token_of)
    feats = feat_ref[...].reshape(sl * tl, feat_ref.shape[2])
    lane_of = lax.broadcasted_iota(jnp.int32, (sl, 128), 1) // pw

    def project(n, w_ref):
        tiled = lax.dot_general(
            w_ref[...], spread, (((0,), (0,)), ((), ())), preferred_element_type=F32
        ).astype(BF16)
        proj[n] = dot(feats, tiled)
        parts = []
        for g in range(spots):
            got = proj[n, pl.ds(g * per, sl, stride=tl), :]
            for t in range(1, per):
                other = proj[n, pl.ds(g * per + t, sl, stride=tl), :]
                got = jnp.where(lane_of == t, other, got)
            parts.append((got * wide_mask[:, g * 128 : (g + 1) * 128]).astype(BF16))
        return parts

    left = project(0, wl_ref)
    right = project(1, wr_ref)
    for k in range(fold):
        for g in range(lgroups):
            lsend[k, 1 + g] = left[k * lgroups + g]
        lsend[k, 0] = jnp.zeros((sl, 128), BF16)
        lsend[k, 0, :, 0:rd] = mask[:, k * rd : (k + 1) * rd]
    for g in range(rgroups):
        rg[row, g] = right[g]
    rg[row, rgroups] = jnp.zeros((sl, 128), BF16)
    rg[row, rgroups, :, 0:tl] = mask

    pl.semaphore_wait(barrier, rn * cn)

    def span(n):
        if isinstance(n, int) and n == 0:
            return pl.ds(0, cgroups + 1)
        return pl.ds(1 + n * cgroups, cgroups)

    def l1_target(k):
        to_row, to_col = col * fold + k, row % cn
        return to_row, to_col, jnp.logical_and(to_row == row, to_col == col)

    def send_left(n):
        for k in range(fold):
            to_row, to_col, mine = l1_target(k)
            slot = row // cn
            src, dst = lsend.at[k, span(n)], lg.at[row, span(n)]

            @pl.when(mine)
            def _():
                pltpu.make_async_copy(src, dst, l1_recv.at[slot, n]).start()

            @pl.when(jnp.logical_not(mine))
            def _():
                remote(src, dst, l1_send.at[k, n], l1_recv.at[slot, n], to_row, to_col).start()

    def spread_left(n):
        for m in range(fold):
            piece = lg.at[col + m * cn, span(n)]
            pltpu.make_async_copy(piece, piece, l1_recv.at[m, n]).wait()
            for d in range(1, cn):
                remote(
                    piece, piece, l2_send.at[m, d - 1, n], l2_recv.at[m, d - 1, n],
                    row, (col + d) % cn,
                ).start()

    def take_left(n):
        for m in range(fold):
            for d in range(1, cn):
                piece = lg.at[(col + cn - d) % cn + m * cn, span(n)]
                pltpu.make_async_copy(piece, piece, l2_recv.at[m, d - 1, n]).wait()

    send_left(0)

    def chain(t):
        low, high = jnp.maximum(row - t, 0), jnp.minimum(row + t, rn - 1)
        ups = jnp.logical_and(row - t >= 0, row + 1 < rn)
        downs = jnp.logical_and(row + t < rn, row >= 1)
        return (ups, low, row + 1), (downs, high, row - 1)

    cut = rgroups // 2
    pieces = (pl.ds(0, cut), pl.ds(cut, rgroups + 1 - cut))

    def pass_on(t):
        for way, (go, slot, to_row) in enumerate(chain(t)):

            @pl.when(go)
            def _():
                for e, piece in enumerate(pieces):
                    part_of = rg.at[slot, piece]
                    remote(
                        part_of, part_of, r_send.at[way, t, e], r_recv.at[slot, e], to_row, col
                    ).start()

    pass_on(0)
    for n in range(1, steps):
        send_left(n)

    tokens = valid_ref.shape[1]
    valid = valid_ref[...].astype(F32)

    def as_rows(first, count):
        hit = lax.broadcasted_iota(jnp.int32, (count, tokens), 1) == first + (
            lax.broadcasted_iota(jnp.int32, (count, tokens), 0)
        )
        chosen = jnp.where(hit, jnp.broadcast_to(valid, (count, tokens)), 0.0).astype(BF16)
        return dot(chosen, jnp.ones((tokens, ch), BF16))

    vrows[0:rd] = as_rows(row * rd, rd)
    valid_cols = as_rows(col * cd, cd)

    loads[1].wait()
    wof[...] = wo_ref[...].astype(F32)
    w4[...] = jnp.zeros_like(w4)
    for q in range(pw):
        part = wof[pl.ds(q, pw, stride=pw), :].astype(BF16)
        for i in range(per):
            w4[q * 128 + i * pw : q * 128 + (i + 1) * pw, i * ch : (i + 1) * ch] = part

    spread_left(0)
    for t in range(rn - 1):
        for e, piece in enumerate(pieces):
            for way, (there_is, slot) in enumerate((
                (row - t - 1 >= 0, jnp.maximum(row - t - 1, 0)),
                (row + t + 1 < rn, jnp.minimum(row + t + 1, rn - 1)),
            )):

                @pl.when(there_is)
                def _():
                    part_of = rg.at[slot, piece]
                    pltpu.make_async_copy(part_of, part_of, r_recv.at[slot, e]).wait()

                if t + 1 < rn - 1:
                    go, _slot, to_row = chain(t + 1)[way]

                    @pl.when(go)
                    def _():
                        part_of = rg.at[slot, piece]
                        remote(
                            part_of, part_of, r_send.at[way, t + 1, e], r_recv.at[slot, e],
                            to_row, col,
                        ).start()

    for n in range(1, steps):
        spread_left(n)
    for g in range(rgroups):
        slab = rg[:, g].astype(F32).reshape(depth, 128)
        rt[g * 128 : (g + 1) * 128, :] = slab.T
    for q in range(pw):
        rq[q * cd : (q + 1) * cd, :] = rt[pl.ds(q, cd, stride=pw), :].astype(BF16)

    take_left(0)
    left_mask = lg[:, 0].astype(F32).reshape(depth, 128)
    right_mask = rg[:, rgroups].astype(F32).reshape(depth, 128)
    counts = dot(right_mask.T.astype(BF16), left_mask.astype(BF16))
    inverse = 1.0 / jnp.maximum(counts, 1.0)
    for i in range(rd):
        rexp[i] = jnp.broadcast_to(inverse[0:cd, i : i + 1], (cd, ch))

    for n in (0, 2, 3, 4, 5):
        loads[n].wait()

    qstep = min(8, pw)

    part = cr // 2

    def to_mirror(step, k, p):
        begin = step * cr + p * part
        src = two.at[pl.ds(begin, part), pl.ds(k * rd, rd)]
        dst = mirror.at[pl.ds((row % fold) * rd + begin, part)]
        return src, dst

    def send_mirror(step, k, p):
        to_row, to_col = col * fold + k, row // fold
        mine = jnp.logical_and(to_row == row, to_col == col)
        across = to_col // chans != col // chans
        src, dst = to_mirror(step, k, p)
        rsem = m_recv.at[row % fold, step, p]
        ssem = m_send.at[k, step, p]

        @pl.when(mine)
        def _():
            pltpu.make_async_copy(src, dst, rsem).start()

        direct = jnp.logical_not(mine)
        if p == 1:
            direct = jnp.logical_and(direct, jnp.logical_not(across))

            @pl.when(across)
            def _():
                slot, core = to_row // chans, to_row % chans
                remote(
                    src, relay.at[slot, step], ssem, rl_recv.at[slot, step], row,
                    to_col // chans * chans + core,
                ).start()

        @pl.when(direct)
        def _():
            remote(src, dst, ssem, rsem, to_row, to_col).start()

    def relayed(m):
        key = m * chans + col % chans
        from_col, to_row, to_col = key // fold, key, row // fold
        active = jnp.logical_and(
            to_col // chans == col // chans, from_col // chans != to_col // chans
        )
        return active, row, to_row, to_col

    def forward(step):
        for m in range(rn // chans):
            active, from_row, to_row, to_col = relayed(m)

            @pl.when(active)
            def _():
                piece = relay.at[m, step]
                pltpu.make_async_copy(piece, piece, rl_recv.at[m, step]).wait()
                begin = (from_row % fold) * rd + step * cr + part
                remote(
                    piece, mirror.at[pl.ds(begin, part)], rl_send.at[m, step],
                    m_recv.at[from_row % fold, step, 1], to_row, to_col,
                ).start()

    lag = min(1, steps)

    def one_step(step, carry):

        @pl.when(step > 0)
        def _():
            take_left(step)

        for g in range(cgroups):
            slab = lg[:, 1 + step * cgroups + g].astype(F32).reshape(depth, 128)
            lcat[0, :, g * 128 : (g + 1) * 128] = slab.astype(BF16)
        lpart = lcat[0]
        for q0 in range(0, pw, qstep):
            z = dot(rq[q0 * cd : (q0 + qstep) * cd, :], lpart).astype(BF16)
            for q in range(qstep):
                for g in range(cgroups):
                    zs[g * cd : (g + 1) * cd, (q0 + q) * 128 : (q0 + q + 1) * 128] = z[
                        q * cd : (q + 1) * cd, g * 128 : (g + 1) * 128
                    ]
        update = dot(zs[...], w4[...])
        for g in range(cgroups):
            for i in range(per):
                at_row = step * cr + g * per + i
                add = update[g * cd : (g + 1) * cd, i * ch : (i + 1) * ch] * rexp[at_row]
                ones[g * per + i] = (pair_ref[at_row].astype(F32) + add).astype(BF16)
        for p in (1, 0):
            values = ones[p * part : (p + 1) * part].reshape(part * cd, ch).astype(F32)
            centre = jnp.mean(values, axis=-1, keepdims=True)
            shifted = values - centre
            var = jnp.mean(jnp.square(shifted), axis=-1, keepdims=True)
            normed = (shifted * lax.rsqrt(var + epsilon)).astype(BF16)
            gate = dot(normed, wg_ref[...])
            up = dot(normed, wu_ref[...])
            hidden = (gate / (1.0 + jnp.exp(-gate)) * up).astype(BF16)
            result = (values + dot(hidden, wd_ref[...])).astype(BF16)
            two[pl.ds(step * cr + p * part, part)] = result.reshape(part, cd, ch)
            for k in range(fold):
                send_mirror(step, k, p)
            if p == 1:

                @pl.when(step >= lag)
                def _():
                    forward(step - lag)

        return carry

    lax.fori_loop(0, steps, one_step, 0)
    for step in range(steps - lag, steps):
        forward(step)

    for step in range(steps):
        for k in range(fold):
            begin = k * rd + step * cr
            for p in (0, 1):
                piece = mirror.at[pl.ds(begin + p * part, part)]
                pltpu.make_async_copy(piece, piece, m_recv.at[k, step, p]).wait()
            mf[begin * rd : (begin + cr) * rd, :] = (
                mirror[begin : begin + cr].astype(F32).reshape(cr * rd, ch)
            )
            some_cols = valid_cols[begin : begin + cr]

            def one_row(i, carry):
                other = mf[pl.ds(begin * rd + i, cr, stride=rd), :]
                half_sum = (two[i, begin : begin + cr].astype(F32) + other) * 0.5
                sym[i, begin : begin + cr] = half_sum
                masked = half_sum * some_cols * vrows[pl.ds(i, 1), :]
                wide[i + 1, begin : begin + cr, ch : 2 * ch] = masked.astype(BF16)
                if begin == 0:
                    colf[0, pl.ds(i, 1), :] = masked[0:1]
                if begin + cr == cd:
                    colf[1, pl.ds(i, 1), :] = masked[cr - 1 : cr]
                return carry

            lax.fori_loop(0, rd, one_row, 0, unroll=4)

    for n, (a, b) in enumerate(AROUND):
        if b == 0:
            hsend[n, 0:cd] = wide[1 if a < 0 else rd, :, ch : 2 * ch]
        elif a == 0:
            hsend[n, 0:rd] = colf[0 if b < 0 else 1].astype(BF16)
        else:
            corner = colf[0 if b < 0 else 1, 0:1] if a < 0 else colf[0 if b < 0 else 1, rd - 1 : rd]
            hsend[n, 0:16] = jnp.broadcast_to(corner, (16, ch)).astype(BF16)

    def there(a, b):
        r, c = row + a, col + b
        return jnp.logical_and(
            jnp.logical_and(r >= 0, r < rn), jnp.logical_and(c >= 0, c < cn)
        )

    def lines(a, b):
        return cd if b == 0 else (rd if a == 0 else 16)

    for n, (a, b) in enumerate(AROUND):

        @pl.when(there(a, b))
        def _():
            size = lines(a, b)
            remote(
                hsend.at[n, pl.ds(0, size)], hrecv.at[n, pl.ds(0, size)], h_send.at[n],
                h_recv.at[n], row + a, col + b,
            ).start()

    place = lax.broadcasted_iota(jnp.int32, (cd, ch), 0)

    def widen(i, before, after):
        centre = wide[i, :, ch : 2 * ch].astype(F32)
        wide[i, :, 0:ch] = jnp.where(place == 0, before, pltpu.roll(centre, 1, 0)).astype(BF16)
        wide[i, :, 2 * ch : 3 * ch] = jnp.where(
            place == cd - 1, after, pltpu.roll(centre, cd - 1, 0)
        ).astype(BF16)

    def widen_row(i, carry):
        widen(i + 1, 0.0, 0.0)
        return carry

    lax.fori_loop(0, rd, widen_row, 0, unroll=4)

    for n, (a, b) in enumerate(AROUND):

        @pl.when(there(-a, -b))
        def _():
            piece = hrecv.at[n, pl.ds(0, lines(a, b))]
            pltpu.make_async_copy(piece, piece, h_recv.at[n]).wait()

    slot_of = {direction: n for n, direction in enumerate(AROUND)}
    wide[0, :, ch : 2 * ch] = hrecv[slot_of[(1, 0)], 0:cd]
    wide[rd + 1, :, ch : 2 * ch] = hrecv[slot_of[(-1, 0)], 0:cd]
    colf[0] = hrecv[slot_of[(0, 1)], 0:rd].astype(F32)
    colf[1] = hrecv[slot_of[(0, -1)], 0:rd].astype(F32)
    edge = lax.broadcasted_iota(jnp.int32, (16, ch), 0)

    def patch_row(i, carry):
        first = wide[i + 1, 0:16, 0:ch].astype(F32)
        wide[i + 1, 0:16, 0:ch] = jnp.where(
            edge == 0, colf[0, pl.ds(i, 1), :], first
        ).astype(BF16)
        last = wide[i + 1, cd - 16 : cd, 2 * ch : 3 * ch].astype(F32)
        wide[i + 1, cd - 16 : cd, 2 * ch : 3 * ch] = jnp.where(
            edge == 15, colf[1, pl.ds(i, 1), :], last
        ).astype(BF16)
        return carry

    lax.fori_loop(0, rd, patch_row, 0, unroll=4)
    widen(
        0,
        hrecv[slot_of[(1, 1)], 0:16].astype(F32)[0:1],
        hrecv[slot_of[(1, -1)], 0:16].astype(F32)[0:1],
    )
    widen(
        rd + 1,
        hrecv[slot_of[(-1, 1)], 0:16].astype(F32)[0:1],
        hrecv[slot_of[(-1, -1)], 0:16].astype(F32)[0:1],
    )

    strip = 8

    def conv(n, carry):
        total = sym[pl.ds(n * strip, strip)].reshape(strip * cd, ch)
        for a in range(3):
            window = wide[pl.ds(n * strip + a, strip)].reshape(strip * cd, 3 * ch)
            total = total + dot(window, wk_ref[a])
        out_ref[pl.ds(n * strip, strip)] = total.astype(BF16).reshape(strip, cd, ch)
        return carry

    lax.fori_loop(0, rd // strip, conv, 0)

    for k in range(fold):
        @pl.when(jnp.logical_not(l1_target(k)[2]))
        def _():
            for n in range(steps):
                piece = lsend.at[k, span(n)]
                pltpu.make_async_copy(piece, piece, l1_send.at[k, n]).wait()

        to_row, to_col = col * fold + k, row // fold

        @pl.when(jnp.logical_not(jnp.logical_and(to_row == row, to_col == col)))
        def _():
            for step in range(steps):
                for p in (0, 1):
                    src, _dst = to_mirror(step, k, p)
                    pltpu.make_async_copy(src, src, m_send.at[k, step, p]).wait()

    for m in range(rn // chans):

        @pl.when(relayed(m)[0])
        def _():
            for step in range(steps):
                piece = relay.at[m, step]
                pltpu.make_async_copy(piece, piece, rl_send.at[m, step]).wait()

    for t in range(rn - 1):
        for way, (go, slot, _to_row) in enumerate(chain(t)):

            @pl.when(go)
            def _():
                for e, piece in enumerate(pieces):
                    part_of = rg.at[slot, piece]
                    pltpu.make_async_copy(part_of, part_of, r_send.at[way, t, e]).wait()

    for m in range(fold):
        for d in range(1, cn):
            for n in range(steps):
                piece = lg.at[col + m * cn, span(n)]
                pltpu.make_async_copy(piece, piece, l2_send.at[m, d - 1, n]).wait()
    for n, (a, b) in enumerate(AROUND):

        @pl.when(there(a, b))
        def _():
            piece = hsend.at[n, pl.ds(0, lines(a, b))]
            pltpu.make_async_copy(piece, piece, h_send.at[n]).wait()


def on_device(
    mesh_shape,
    pair_input,
    alignment_features,
    alignment_mask,
    token_valid,
    left_weight,
    right_weight,
    output_weight,
    gate_weight,
    up_weight,
    down_weight,
    kernel_weight,
):
    rd, cd, ch = pair_input.shape
    sl, tl, aw = alignment_features.shape
    pw = left_weight.shape[1]
    hid = gate_weight.shape[1]
    rn, chans = mesh_shape["row"], mesh_shape["chan"]
    cn = mesh_shape["col"] * chans
    fold = rn // cn
    per = 128 // pw
    cr = min(16, rd)
    depth = rn * sl
    steps = rd // cr
    tall = max(rd, cd, 16)
    wk = kernel_weight.reshape(3, 3 * ch, ch)
    sizes = (rn, cn, chans, fold, rd, cd, ch, sl, tl, pw, cr)
    large = (pair_input, output_weight, gate_weight, up_weight, down_weight, wk)
    dma = pltpu.SemaphoreType.DMA
    vmem = pl.BlockSpec(memory_space=pltpu.VMEM)
    return pl.pallas_call(
        functools.partial(block_kernel, sizes),
        out_shape=jax.ShapeDtypeStruct((rd, cd, ch), BF16),
        in_specs=[vmem] * 5 + [pl.BlockSpec(memory_space=pl.ANY)] * 6,
        out_specs=vmem,
        scratch_shapes=[
            *[pltpu.VMEM(value.shape, value.dtype) for value in large],
            dma((6,)),
            pltpu.VMEM((2, sl * tl, 128), F32),
            pltpu.VMEM((tall, ch), F32),
            pltpu.VMEM((fold, rd // per + 1, sl, 128), BF16),
            pltpu.VMEM((rn, rd // per + 1, sl, 128), BF16),
            pltpu.VMEM((rn, cd // per + 1, sl, 128), BF16),
            pltpu.VMEM((cd * pw, depth), F32),
            pltpu.VMEM((pw * cd, depth), BF16),
            pltpu.VMEM((1, depth, cr * pw), BF16),
            pltpu.VMEM((pw * pw, ch), F32),
            pltpu.VMEM((pw * 128, per * ch), BF16),
            pltpu.VMEM((cr // per * cd, pw * 128), BF16),
            pltpu.VMEM((rd, cd, ch), F32),
            pltpu.VMEM((cr, cd, ch), BF16),
            pltpu.VMEM((rd, cd, ch), BF16),
            pltpu.VMEM((cd, rd, ch), BF16),
            pltpu.VMEM((cd * rd, ch), F32),
            pltpu.VMEM((rd, cd, ch), F32),
            pltpu.VMEM((rd + 2, cd, 3 * ch), BF16),
            pltpu.VMEM((2, rd, ch), F32),
            pltpu.VMEM((8, tall, ch), BF16),
            pltpu.VMEM((8, tall, ch), BF16),
            dma((fold, steps)),
            dma((fold, steps)),
            dma((fold, cn - 1, steps)),
            dma((fold, cn - 1, steps)),
            dma((2, rn - 1, 2)),
            dma((rn, 2)),
            dma((fold, steps, 2)),
            dma((fold, steps, 2)),
            pltpu.VMEM((rn // chans, steps, cr // 2, rd, ch), BF16),
            dma((rn // chans, steps)),
            dma((rn // chans, steps)),
            dma((8,)),
            dma((8,)),
        ],
        compiler_params=pltpu.CompilerParams(
            collective_id=0, has_side_effects=True, vmem_limit_bytes=60 * 1024 * 1024
        ),
    )(
        alignment_features,
        alignment_mask,
        token_valid.reshape(1, -1),
        left_weight.T,
        right_weight.T,
        *large,
    )


def solution(mesh):
    placed = (
        P(("groups", "row"), ("col", "chan"), None),
        P("row", ("groups", "col", "chan"), None),
        P("row", ("groups", "col", "chan")),
        P("groups"),
        P(),
        P(),
        P(),
        P(),
        P(),
        P(),
        P(),
    )
    return jax.shard_map(
        functools.partial(on_device, dict(mesh.shape)),
        mesh=mesh,
        in_specs=placed,
        out_specs=P(("groups", "row"), ("col", "chan"), None),
        check_vma=False,
    )
```
